512 devices in a mesh: pb: 16 (over y_hi, x, core), lab: 32 (over y_lo, z).
Axes of the slice: x: 4, y: 4 (y_hi: 2, y_lo: 2; y = y_hi * 2 + y_lo), z: 16, core: 2. Of those that a mesh axis runs over, the one named last changes fastest.
Arguments:
- queries: bfloat16 [16384, 768], P(('pb', 'lab')), may hold values from -6 to 6
- label_weights: bfloat16 [32768, 768], P('lab'), may hold values from -0.21875 to 0.21875
- sibling_blocks: int32 [16384, 8], P('pb'), may hold values from 0 to 255, as said below
- positive_slot: int32 [16384], P('pb'), may hold values from 0 to 1023
Outputs:
- query_grad: float32 [16384, 768], P(('pb', 'lab'))
- weight_grad: bfloat16 [32768, 768], P('lab')
The draws below stay inside these ranges and needn't reach their ends.
Inputs may be any that keep to these rules, and one draw needn't show every extreme that they name: `sibling_blocks`: each row names 8 different cluster blocks, lying in 8 different runs of 8 blocks (block // 8 differs). Rows are taken in aligned runs of 32 (one device's queries): within each run, exactly 8 rows name a block of each run of 8 blocks. Within each query group (aligned blocks of 1024 rows) no block is named by more than 144 rows, and some block is named by exactly 144 rows.
All inputs are finite; a program needn't handle non-finite values.
Results may differ from the reference program's by a relative error of at most 0.0047.
Values may be sent and summed in bfloat16 or wider, within the bound.
A program may use at most 64 MiB of HBM per device.

```python
import jax
import jax.numpy as jnp
from jax import lax

D = 768
BLOCK = 128
K = 8
Q_DEV = 32
BPD = 8
GROUPS = 16
Q_GRP = 1024
NQ = 16384
NB = 256
L = 32768
CAP = 144
N_LAB = 32


def draw_sibling_blocks(key, part):
    key_off, key_rows, key_blk = jax.random.split(key, 3)
    offset = jax.random.randint(key_off, (GROUPS, N_LAB, 1, 1), 0, N_LAB)
    row_keys = jax.random.split(key_rows, GROUPS * N_LAB)
    row_perm = jax.vmap(lambda one: jax.random.permutation(one, Q_DEV))(row_keys)
    row_perm = row_perm.reshape(GROUPS, N_LAB, Q_DEV, 1).astype(jnp.int32)
    steps_k = jnp.arange(K, dtype=jnp.int32).reshape(1, 1, 1, K)
    device = (offset + row_perm * K + steps_k) % N_LAB
    home = jnp.arange(N_LAB, dtype=jnp.int32).reshape(1, N_LAB, 1, 1)
    pick = jnp.broadcast_to(jnp.minimum(home % (2 * BPD), BPD - 1), device.shape)
    blk_keys = jax.random.split(key_blk, GROUPS * N_LAB)
    blk_perm = jax.vmap(lambda one: jax.random.permutation(one, BPD))(blk_keys)
    blk_perm = blk_perm.reshape(GROUPS, N_LAB, BPD).astype(jnp.int32)
    group_idx = jnp.broadcast_to(jnp.arange(GROUPS, dtype=jnp.int32).reshape(GROUPS, 1, 1, 1), device.shape)
    local = blk_perm[group_idx, device, pick]
    return (device * BPD + local).reshape(NQ, K).astype(jnp.int32)


def with_ends(result, stream_key, smallest, high):
    extent = result.shape
    place = [jax.random.randint(jax.random.fold_in(stream_key, axis), (), 0, extent[axis]) for axis in range(len(extent))]
    result = result.at[tuple(place)].set(smallest)
    longest = extent.index(max(extent))
    place[longest] = (place[longest] + 1) % extent[longest]
    return result.at[tuple(place)].set(high)


def level_of(key, dims, shards, smallest, largest):
    gain, own = 1.0, jax.random.fold_in(key, 6)
    for dim, shards_of in shards:
        heights = jnp.exp(jax.random.uniform(jax.random.fold_in(own, dim), (shards_of,), jnp.float32, smallest / len(shards), largest / len(shards)))
        gain = gain * jnp.repeat(heights, dims[dim] // shards_of).reshape([-1 if axis == dim else 1 for axis in range(len(dims))])
    return gain


def noise(own_key, extent, spread, most, cuts=(), held_as=jnp.bfloat16):
    gain = level_of(own_key, extent, cuts, -0.22, 0.18) if cuts else 1.0
    array = jax.random.normal(own_key, extent, jnp.float32) * spread * gain
    return jnp.minimum(jnp.maximum(array, -most), most).astype(held_as)


def setup_inputs(seed: int = 0) -> dict:
    splits = jax.random.split(jax.random.key(seed), 5)
    return {
        "queries": noise(splits[0], (NQ, D), 1.0, 6.0, ((0, 512),)),
        "label_weights": noise(splits[1], (L, D), D ** -0.5, 0.21875, ((0, 32),)),
        "sibling_blocks": draw_sibling_blocks(jax.random.fold_in(splits[4], 71), 0),
        "positive_slot": with_ends(jax.random.randint(splits[3], (NQ,), 0, K * BLOCK), jax.random.fold_in(splits[3], 1), 0, (K * BLOCK) - 1).astype(jnp.int32),
    }


def group_terms(q_grp, sel_grp, pos_grp, w_blocks):
    nblk = w_blocks.shape[0]
    qcount = q_grp.shape[0]
    block_ids = jnp.arange(nblk, dtype=jnp.int32)
    hit = jnp.any(sel_grp[:, :, None] == block_ids[None, None, :], axis=1).astype(jnp.int32)
    rank = jnp.cumsum(hit, axis=0) - 1
    slot = jnp.take_along_axis(rank, sel_grp, axis=1)
    query_ids = jnp.broadcast_to(jnp.arange(qcount, dtype=jnp.int32)[:, None], sel_grp.shape)
    table = jnp.zeros((nblk, CAP), jnp.int32).at[sel_grp, slot].set(query_ids)
    valid = jnp.zeros((nblk, CAP), jnp.float32).at[sel_grp, slot].set(1.0)
    pblock = jnp.take_along_axis(sel_grp, (pos_grp // BLOCK)[:, None], axis=1)[:, 0]
    positive = pblock * BLOCK + pos_grp % BLOCK
    rows = q_grp[table].astype(jnp.float32)
    wide_w = w_blocks.astype(jnp.float32)
    scores = jnp.einsum('bcd,bld->bcl', rows, wide_w)
    label_ids = block_ids[:, None] * BLOCK + jnp.arange(BLOCK, dtype=jnp.int32)[None, :]
    target = (label_ids[:, None, :] == positive[table][:, :, None]).astype(jnp.float32)
    slope = (valid[:, :, None] * (jax.nn.sigmoid(scores) - target)).astype(jnp.bfloat16).astype(jnp.float32)
    w_part = jnp.einsum('bcl,bcd->bld', slope, rows)
    dq_parts = jnp.einsum('bcl,bld->bcd', slope, wide_w)
    dq = jnp.zeros((qcount, q_grp.shape[1]), jnp.float32).at[table].add(dq_parts)
    return dq, w_part.reshape(nblk * BLOCK, q_grp.shape[1])


def reference(queries, label_weights, sibling_blocks, positive_slot):
    qs = queries.reshape(GROUPS, Q_GRP, D)
    sels = sibling_blocks.reshape(GROUPS, Q_GRP, K)
    poss = positive_slot.reshape(GROUPS, Q_GRP)
    w_blocks = label_weights.reshape(NB, BLOCK, D)

    def step(w_sum, items):
        dq, w_part = group_terms(items[0], items[1], items[2], w_blocks)
        return w_sum + w_part, dq

    w_sum, dqs = lax.scan(step, jnp.zeros((L, D), jnp.float32), (qs, sels, poss))
    return dqs.reshape(NQ, D), (w_sum / GROUPS).astype(jnp.bfloat16)
```

```python
import functools

import jax
import jax.numpy as jnp
from jax import lax
from jax.experimental import pallas as pl
from jax.experimental.pallas import tpu as pltpu
from jax.sharding import PartitionSpec as P

MESH = pl.DeviceIdType.MESH
BLOCK = 128
F32 = jnp.float32
BF16 = jnp.bfloat16


def mm(a, b, ca=1, cb=0):
    return lax.dot_general(a, b, (((ca,), (cb,)), ((), ())), preferred_element_type=F32)


def kernel(n_pb, n_lab, q_ref, w_ref, sib_ref, pos_ref, dq_ref, wg_ref, sbuf, rbuf, xbuf, pown, meta, meta_x, sbuf2, rbuf2,
           dwbuf, dwrecv, fin, s1, r1, sx, rx, s2, r2, s3, r3, s4, r4, s5, r5):
    runs, rows = sib_ref.shape[1], sib_ref.shape[2]
    kk = sib_ref.shape[0]
    cap = rows * kk // n_lab
    slots = n_lab * cap
    dim = q_ref.shape[1]
    labels = w_ref.shape[0]
    nblk = labels // BLOCK
    half = labels // 2
    chips = n_pb // 2
    piece = half // chips
    nz = n_lab // 2
    p = lax.axis_index("pb")
    me = lax.axis_index("lab")
    core = lax.rem(p, 2)
    chip = lax.div(p, 2)
    partner = p + 1 - 2 * core
    my_y = lax.div(me, nz)
    my_z = lax.rem(me, nz)

    def peer(t):
        back = n_lab - 1 - t
        step = lax.div(back, 2)
        dist = lax.div(step + 1, 2)
        dz = jnp.where(lax.rem(step, 2) == 1, dist, -dist)
        z = lax.rem(my_z + dz + nz, nz)
        y = lax.rem(my_y + lax.rem(back, 2), 2)
        return y * nz + z

    barrier = pltpu.get_barrier_semaphore()
    pl.semaphore_signal(barrier, inc=1, device_id=(partner, me), device_id_type=MESH)

    def sig_lab(t, c):
        pl.semaphore_signal(barrier, inc=1, device_id=(p, peer(t)), device_id_type=MESH)
        return c

    lax.fori_loop(0, n_lab - 1, sig_lab, 0)

    def sig_pb(t, c):
        other = lax.rem(chip + t, chips)
        pl.semaphore_signal(barrier, inc=1, device_id=(2 * other + core, me), device_id_type=MESH)
        return c

    lax.fori_loop(1, chips, sig_pb, 0)

    iota = lambda shape, ax: lax.broadcasted_iota(jnp.int32, shape, ax)
    expand = (iota((slots, n_lab), 0) // cap == iota((slots, n_lab), 1)).astype(BF16)
    upper = (iota((rows, rows), 0) <= iota((rows, rows), 1)).astype(BF16)
    rank_want = (lax.rem(iota((slots, rows), 0), cap) + 1).astype(F32)

    def pick(hit):
        hit_b = hit.astype(BF16)
        rank = mm(hit_b, upper)
        hx = mm(expand, hit_b)
        rx_ = mm(expand, rank.astype(BF16))
        return jnp.logical_and(hx > 0.5, rx_ == rank_want)

    run_id = iota((n_lab, rows), 0)
    hit_own = jnp.zeros((n_lab, rows), F32)
    for k in range(kk):
        row = sib_ref[k, pl.ds(me, 1), :]
        hit_own = jnp.where(jnp.right_shift(row, 3) == run_id, 1.0, hit_own)
    sel_own = jnp.where(pick(hit_own), 1.0, 0.0).astype(BF16)
    pown[...] = sel_own
    sent = mm(sel_own, q_ref[...])
    sbuf[...] = sent.reshape(n_lab, cap, dim).astype(BF16)

    pl.semaphore_wait(barrier, n_lab - 1 + chips - 1 + 1)

    def copy1(to, src_of):
        return pltpu.make_async_remote_copy(
            src_ref=sbuf.at[to], dst_ref=rbuf.at[src_of], send_sem=s1.at[to], recv_sem=r1.at[src_of],
            device_id=(p, to), device_id_type=MESH)

    def send1(t, c):
        copy1(peer(t), me).start()
        return c

    lax.fori_loop(0, n_lab - 1, send1, 0)
    rbuf[pl.ds(me, 1)] = sbuf[pl.ds(me, 1)]

    pos = pos_ref[...]
    hit_lab = jnp.zeros((runs, rows), F32)
    blk = jnp.zeros((runs, rows), F32)
    pblock = jnp.zeros((runs, rows), jnp.int32)
    for k in range(kk):
        sk = sib_ref[k]
        mine = jnp.right_shift(sk, 3) == me
        hit_lab = jnp.where(mine, 1.0, hit_lab)
        blk = jnp.where(mine, jnp.bitwise_and(sk, 7).astype(F32), blk)
        pblock = jnp.where(jnp.right_shift(pos, 7) == k, sk, pblock)
    pcol = jnp.where(jnp.right_shift(pblock, 3) == me, jnp.bitwise_and(pos, BLOCK - 1), -1).astype(F32)
    sel_lab = pick(hit_lab)
    blk_s = jnp.sum(jnp.where(sel_lab, mm(expand, blk.astype(BF16)), 0.0), axis=1, keepdims=True)
    pc_s = jnp.sum(jnp.where(sel_lab, mm(expand, pcol.astype(BF16)), 0.0), axis=1, keepdims=True)
    lane = iota((slots, BLOCK), 1)
    meta[...] = jnp.where(lane == 0, blk_s, pc_s)
    fwd_meta = pltpu.make_async_remote_copy(
        src_ref=meta, dst_ref=meta_x, send_sem=sx.at[0], recv_sem=rx.at[0], device_id=(partner, me), device_id_type=MESH)
    fwd_meta.start()

    def wait1(t, c):
        copy1(peer(t), peer(t)).wait_recv()
        return c

    lax.fori_loop(0, n_lab - 1, wait1, 0)
    fwd_rows = pltpu.make_async_remote_copy(
        src_ref=rbuf, dst_ref=xbuf, send_sem=sx.at[1], recv_sem=rx.at[1], device_id=(partner, me), device_id_type=MESH)
    fwd_rows.start()

    lane_f = lane.astype(F32)

    def slope128(x, w, b_of, pc, n):
        scores = mm(x, w, 1, 1)
        acc = jnp.zeros((slots, BLOCK), F32)
        for b in range(n):
            acc = jnp.where(b_of == float(b), scores[:, b * BLOCK:(b + 1) * BLOCK], acc)
        return jax.nn.sigmoid(acc) - jnp.where(lane_f == pc, 1.0, 0.0)

    def spread(sl, b_of, n):
        return jnp.concatenate([jnp.where(b_of == float(b), sl, 0.0) for b in range(n)], axis=1).astype(BF16)

    x = rbuf[...].astype(F32).reshape(slots, dim).astype(BF16)
    sl = slope128(x, w_ref[...], blk_s, pc_s, nblk)
    dq_part = mm(spread(sl, blk_s, nblk), w_ref[...])
    sbuf2[...] = dq_part.reshape(n_lab, cap, dim).astype(BF16)

    def copy2(to, src_of):
        return pltpu.make_async_remote_copy(
            src_ref=sbuf2.at[to], dst_ref=rbuf2.at[src_of], send_sem=s2.at[to], recv_sem=r2.at[src_of],
            device_id=(p, to), device_id_type=MESH)

    def send2(t, c):
        copy2(peer(t), me).start()
        return c

    lax.fori_loop(0, n_lab - 1, send2, 0)
    rbuf2[pl.ds(me, 1)] = sbuf2[pl.ds(me, 1)]

    hblk = nblk // 2
    first = core.astype(F32) * hblk
    own_half = spread(sl, blk_s - first, hblk)
    dw = mm(own_half, x, 0, 0)
    fwd_meta.wait_recv()
    fwd_rows.wait_recv()
    x2 = xbuf[...].astype(F32).reshape(slots, dim).astype(BF16)
    m2 = meta_x[...]
    b2 = m2[:, 0:1] - first
    pc2 = m2[:, 1:2]
    w_half = w_ref[pl.ds(pl.multiple_of(core * half, half), half), :]
    sl2 = slope128(x2, w_half, b2, pc2, hblk)
    dw = dw + mm(spread(sl2, b2, hblk), x2, 0, 0)
    dwbuf[...] = dw.astype(BF16).reshape(chips, piece, dim)

    def copy3(to, src_of):
        return pltpu.make_async_remote_copy(
            src_ref=dwbuf.at[to], dst_ref=dwrecv.at[src_of], send_sem=s3.at[to], recv_sem=r3.at[src_of],
            device_id=(2 * to + core, me), device_id_type=MESH)

    def send3(t, c):
        copy3(lax.rem(chip + t, chips), chip).start()
        return c

    lax.fori_loop(1, chips, send3, 0)
    dwrecv[pl.ds(chip, 1)] = dwbuf[pl.ds(chip, 1)]

    def wait3(t, c):
        other = lax.rem(chip + t, chips)
        copy3(other, other).wait_recv()
        return c

    lax.fori_loop(1, chips, wait3, 0)
    total = dwrecv[0].astype(F32)
    for j in range(1, chips):
        total = total + dwrecv[j].astype(F32)
    done = (total / n_pb).astype(BF16)
    fin[...] = done

    def rows_of(c_, j):
        return pl.ds(pl.multiple_of(c_ * half + j * piece, piece), piece)

    wg_ref[rows_of(core, chip), :] = done

    def copy4(to, src_of):
        return pltpu.make_async_remote_copy(
            src_ref=fin, dst_ref=wg_ref.at[rows_of(core, src_of)], send_sem=s4.at[to], recv_sem=r4.at[src_of],
            device_id=(2 * to + core, me), device_id_type=MESH)

    def send4(t, c):
        copy4(lax.rem(chip + t, chips), chip).start()
        return c

    lax.fori_loop(1, chips, send4, 0)
    to_partner = pltpu.make_async_remote_copy(
        src_ref=fin, dst_ref=wg_ref.at[rows_of(core, chip)], send_sem=s5.at[chip], recv_sem=r5.at[chip],
        device_id=(partner, me), device_id_type=MESH)
    to_partner.start()

    def wait2(t, c):
        copy2(peer(t), peer(t)).wait_recv()
        return c

    lax.fori_loop(0, n_lab - 1, wait2, 0)
    back = rbuf2[...].astype(F32).reshape(slots, dim).astype(BF16)
    dq_ref[...] = mm(pown[...], back, 0, 0)

    def copy5(c_, j):
        return pltpu.make_async_remote_copy(
            src_ref=wg_ref.at[rows_of(c_, j)], dst_ref=wg_ref.at[rows_of(c_, j)], send_sem=s5.at[j], recv_sem=r5.at[j],
            device_id=(partner, me), device_id_type=MESH)

    def relay(t, c):
        other = lax.rem(chip + t, chips)
        copy4(other, other).wait_recv()
        copy5(core, other).start()
        return c

    lax.fori_loop(1, chips, relay, 0)

    def wait5(j, c):
        copy5(1 - core, j).wait_recv()
        return c

    lax.fori_loop(0, chips, wait5, 0)

    def drain_lab(t, c):
        copy1(peer(t), me).wait_send()
        copy2(peer(t), me).wait_send()
        return c

    lax.fori_loop(0, n_lab - 1, drain_lab, 0)

    def drain_pb(t, c):
        other = lax.rem(chip + t, chips)
        copy3(other, chip).wait_send()
        copy4(other, chip).wait_send()
        copy5(core, other).wait_send()
        return c

    lax.fori_loop(1, chips, drain_pb, 0)
    to_partner.wait_send()
    fwd_meta.wait_send()
    fwd_rows.wait_send()


def shards(n_pb, n_lab, queries, label_weights, sibling_blocks, positive_slot):
    rows, dim = queries.shape
    labels = label_weights.shape[0]
    kk = sibling_blocks.shape[1]
    runs = sibling_blocks.shape[0] // rows
    cap = rows * kk // n_lab
    slots = n_lab * cap
    chips = n_pb // 2
    piece = labels // 2 // chips
    sib = sibling_blocks.T.reshape(kk, runs, rows)
    pos = positive_slot.reshape(runs, rows)
    vmem = pl.BlockSpec(memory_space=pltpu.VMEM)
    dma = pltpu.SemaphoreType.DMA
    packets = pltpu.VMEM((n_lab, cap, dim), BF16)
    return pl.pallas_call(
        functools.partial(kernel, n_pb, n_lab),
        out_shape=(jax.ShapeDtypeStruct((rows, dim), F32), jax.ShapeDtypeStruct((labels, dim), BF16)),
        in_specs=[vmem] * 4,
        out_specs=(vmem, vmem),
        scratch_shapes=[
            packets, packets, packets, pltpu.VMEM((slots, rows), BF16),
            pltpu.VMEM((slots, BLOCK), F32), pltpu.VMEM((slots, BLOCK), F32), packets, packets,
            pltpu.VMEM((chips, piece, dim), BF16), pltpu.VMEM((chips, piece, dim), BF16), pltpu.VMEM((piece, dim), BF16),
            dma((n_lab,)), dma((n_lab,)), dma((2,)), dma((2,)), dma((n_lab,)), dma((n_lab,)),
            dma((chips,)), dma((chips,)), dma((chips,)), dma((chips,)), dma((chips,)), dma((chips,)),
        ],
        compiler_params=pltpu.CompilerParams(collective_id=0, has_side_effects=True),
    )(queries, label_weights, sib, pos)


def solution(mesh):
    in_specs = (P(("pb", "lab"), None), P("lab", None), P("pb", None), P("pb"))
    out_specs = (P(("pb", "lab"), None), P("lab", None))
    body = functools.partial(shards, mesh.shape["pb"], mesh.shape["lab"])
    return jax.shard_map(body, mesh=mesh, in_specs=in_specs, out_specs=out_specs, check_vma=False)
```

```python
import functools

import jax
import jax.numpy as jnp
from jax import lax
from jax.experimental import pallas as pl
from jax.experimental.pallas import tpu as pltpu
from jax.sharding import PartitionSpec as P

MESH = pl.DeviceIdType.MESH
BLOCK = 128
HOP = 4
LIST = 16
F32 = jnp.float32
BF16 = jnp.bfloat16
SELF_NEAR = 2 * (HOP - 1)
N_NEAR = 2 * (2 * HOP - 1)
N_RELAY = 2 * HOP + 1


def mm(a, b, ca=1, cb=0):
    return lax.dot_general(a, b, (((ca,), (cb,)), ((), ())), preferred_element_type=F32)


def iota(shape, ax):
    return lax.broadcasted_iota(jnp.int32, shape, ax)


def kernel(n_pb, n_lab, q_ref, w_hbm, sib_ref, pos_ref, dq_ref, wg_ref, w_ref, sbuf, fbuf, relbuf, rbuf, xbuf, pown, prel, meta, meta_x,
           sbuf2, nbuf, rrbuf, fsend, fback, dwbuf, dwrecv, fin,
           sw, s1, r1, sf, rf, sr, sx, rx, s2, rn, rr, sb, rb, s3, r3, s4, r4, s5, r5):
    kk, total_rows = sib_ref.shape
    rows, dim = q_ref.shape
    cap = rows * kk // n_lab
    slots = n_lab * cap
    labels = w_hbm.shape[0]
    nblk = labels // BLOCK
    half = labels // 2
    chips = n_pb // 2
    piece = half // chips
    nz = n_lab // 2
    p = lax.axis_index("pb")
    me = lax.axis_index("lab")
    core = lax.rem(p, 2)
    chip = lax.div(p, 2)
    partner = p + 1 - 2 * core
    my_y = lax.div(me, nz)
    my_z = lax.rem(me, nz)

    def at(dy, dz):
        return lax.rem(my_y + dy, 2) * nz + lax.rem(my_z + dz + nz, nz)

    load_w = pltpu.make_async_copy(w_hbm, w_ref, sw)
    load_w.start()

    barrier = pltpu.get_barrier_semaphore()
    for dz in range(-HOP, HOP + 1):
        for dy in range(2):
            if dz or dy:
                pl.semaphore_signal(barrier, inc=1, device_id=(p, at(dy, dz)), device_id_type=MESH)
    pl.semaphore_signal(barrier, inc=1, device_id=(partner, me), device_id_type=MESH)
    for t in range(1, chips):
        pl.semaphore_signal(barrier, inc=1, device_id=(2 * lax.rem(chip + t, chips) + core, me), device_id_type=MESH)

    src_a, src_b = at(0, -HOP), at(0, HOP)
    upper = (iota((rows, rows), 0) <= iota((rows, rows), 1)).astype(BF16)

    def pick(hit_b, n):
        expand = (iota((n * cap, n), 0) // cap == iota((n * cap, n), 1)).astype(BF16)
        want = (lax.rem(iota((n * cap, rows), 0), cap) + 1).astype(F32)
        rank = mm(hit_b, upper)
        on = mm(expand, hit_b)
        return jnp.logical_and(on > 0.5, mm(expand, rank.astype(BF16)) == want), expand

    sib = sib_ref[...]
    col = iota((total_rows, 3 * rows), 1)
    run_of = jnp.where(col < rows, me, jnp.where(col < 2 * rows, src_a, src_b))
    take = (iota((total_rows, 3 * rows), 0) == run_of * rows + lax.rem(col, rows)).astype(BF16)
    mine3 = mm(sib.astype(BF16), take)

    jrow = iota((LIST, rows), 0)
    jy = lax.rem(jrow, 2)
    jm = lax.div(jrow, 2)

    def lab_of(dy, dz):
        return lax.rem(my_y + dy, 2) * nz + lax.rem(my_z + dz + nz, nz)

    near_ids = jnp.where(jrow < N_NEAR, lab_of(jy, jm - (HOP - 1)), -1)
    ids_a = jnp.where(jrow < N_RELAY, lab_of(jy, jm), -1)
    ids_b = jnp.where(jrow < N_RELAY, lab_of(jnp.where(jrow == N_RELAY - 1, 1, jy), -jm), -1)
    hits = []
    for n, ids in enumerate((near_ids, ids_a, ids_b)):
        hit = jnp.zeros((LIST, rows), F32)
        for k in range(kk):
            blocks = mine3[k:k + 1, n * rows:(n + 1) * rows].astype(jnp.int32)
            hit = jnp.where(jnp.right_shift(blocks, 3) == ids, 1.0, hit)
        hits.append(hit)
    sel3, _ = pick(jnp.concatenate(hits, axis=0).astype(BF16), 3 * LIST)
    sel3 = jnp.where(sel3, 1.0, 0.0).astype(BF16)
    width = LIST * cap
    pown[...] = sel3[:width]
    prel[...] = sel3[width:]
    sbuf[...] = mm(sel3[:width], q_ref[...]).reshape(LIST, cap, dim).astype(BF16)

    pl.semaphore_wait(barrier, 2 * (2 * HOP + 1) - 1 + chips)

    def remote(src, dst, send, recv, dev):
        return pltpu.make_async_remote_copy(
            src_ref=src, dst_ref=dst, send_sem=send, recv_sem=recv, device_id=dev, device_id_type=MESH)

    def chunk_out(s):
        return remote(q_ref, fbuf.at[s], sf.at[s], rf.at[s], (p, at(0, HOP if s == 0 else -HOP)))

    chunk_out(0).start()
    chunk_out(1).start()
    near = [(dz * sg, dy) for dz in range(HOP - 1, -1, -1) for sg in ((1, -1) if dz else (1,)) for dy in (0, 1) if dz or dy]
    for dz, dy in near:
        j = 2 * (dz + HOP - 1) + dy
        remote(sbuf.at[j], rbuf.at[me], s1.at[0], r1, (p, at(dy, dz))).start()
    rbuf[pl.ds(me, 1)] = sbuf[pl.ds(SELF_NEAR, 1)]

    qrow = iota((n_lab, total_rows), 1)
    in_run = jnp.right_shift(qrow, 5) == iota((n_lab, total_rows), 0)
    fold = (jnp.bitwise_and(iota((total_rows, rows), 0), rows - 1) == iota((total_rows, rows), 1)).astype(BF16)
    here = jnp.right_shift(sib, 3) == me
    pos = pos_ref[...]
    blk1 = jnp.sum(jnp.where(here, jnp.bitwise_and(sib, 7) + 1, 0), axis=0, keepdims=True)
    is_pos = jnp.logical_and(here, iota((kk, total_rows), 0) == jnp.right_shift(pos, 7))
    col1 = jnp.sum(jnp.where(is_pos, jnp.bitwise_and(pos, BLOCK - 1) + 1, 0), axis=0, keepdims=True)
    packed = jnp.concatenate([jnp.where(in_run, blk1, 0), jnp.where(in_run, col1, 0)], axis=0)
    table = mm(packed.astype(F32).astype(BF16), fold)
    blk_t, col_t = table[:n_lab], table[n_lab:]
    sel_lab, expand = pick(jnp.where(blk_t > 0.5, 1.0, 0.0).astype(BF16), n_lab)
    blk_s = jnp.sum(jnp.where(sel_lab, mm(expand, blk_t.astype(BF16)), 0.0), axis=1, keepdims=True) - 1.0
    pc_s = jnp.sum(jnp.where(sel_lab, mm(expand, col_t.astype(BF16)), 0.0), axis=1, keepdims=True) - 1.0
    lane = iota((slots, BLOCK), 1)
    meta[...] = jnp.where(lane == 0, blk_s, pc_s)
    fwd_meta = remote(meta, meta_x, sx.at[0], rx.at[0], (partner, me))
    fwd_meta.start()
    nbuf[N_NEAR:] = jnp.zeros((LIST - N_NEAR, cap, dim), BF16)
    rrbuf[0, N_RELAY:] = jnp.zeros((LIST - N_RELAY, cap, dim), BF16)
    rrbuf[1, N_RELAY:] = jnp.zeros((LIST - N_RELAY, cap, dim), BF16)

    def stop(s, jj):
        if jj == N_RELAY - 1:
            return (0, HOP) if s == 0 else (1, -HOP)
        m, dy = divmod(jj, 2)
        return dy, (m if s == 0 else -m)

    srcs = (src_a, src_b)
    for s in range(2):
        chunk_out(s).wait_recv()
        out = mm(prel[s * width:(s + 1) * width], fbuf[s])
        relbuf[s] = out.reshape(LIST, cap, dim).astype(BF16)
        for jj in range(N_RELAY - 1, 0, -1):
            dy, dz = stop(s, jj)
            remote(relbuf.at[s, jj], rbuf.at[srcs[s]], sr.at[s], r1, (p, at(dy, dz))).start()
        rbuf[pl.ds(srcs[s], 1)] = relbuf[s, 0:1]

    def bulk(ref, sem):
        return remote(ref, ref, sem, sem, (partner, me))

    n_in = n_lab - 3
    bulk(rbuf.at[pl.ds(0, n_in)], r1).wait_recv()
    fwd_rows = remote(rbuf, xbuf, sx.at[1], rx.at[1], (partner, me))
    fwd_rows.start()
    load_w.wait()

    lane_f = lane.astype(F32)

    def slope128(x, w, b_of, pc, n):
        scores = mm(x, w, 1, 1)
        acc = jnp.zeros((slots, BLOCK), F32)
        for b in range(n):
            acc = jnp.where(b_of == float(b), scores[:, b * BLOCK:(b + 1) * BLOCK], acc)
        return jax.nn.sigmoid(acc) - jnp.where(lane_f == pc, 1.0, 0.0)

    def spread(sl, b_of, n):
        return jnp.concatenate([jnp.where(b_of == float(b), sl, 0.0) for b in range(n)], axis=1).astype(BF16)

    x = rbuf[...].astype(F32).reshape(slots, dim).astype(BF16)
    sl = slope128(x, w_ref[...], blk_s, pc_s, nblk)
    dq_part = mm(spread(sl, blk_s, nblk), w_ref[...])
    sbuf2[...] = dq_part.reshape(n_lab, cap, dim).astype(BF16)

    for s in range(2):
        for jj in range(N_RELAY - 1, 0, -1):
            dy, dz = stop(s, jj)
            relay_dz = -dz
            home = at(dy, relay_dz - HOP if s == 0 else relay_dz + HOP)
            remote(sbuf2.at[home], rrbuf.at[s, jj], s2, rr.at[s], (p, at(dy, relay_dz))).start()
        rrbuf[s, 0:1] = sbuf2[pl.ds(srcs[s], 1)]
    for dz, dy in near:
        home = at(dy, dz)
        remote(sbuf2.at[home], nbuf.at[2 * (HOP - 1 - dz) + dy], s2, rn, (p, home)).start()
    nbuf[SELF_NEAR:SELF_NEAR + 1] = sbuf2[pl.ds(me, 1)]

    hblk = nblk // 2
    first = core.astype(F32) * hblk
    dw = mm(spread(sl, blk_s - first, hblk), x, 0, 0)
    fwd_meta.wait_recv()
    fwd_rows.wait_recv()
    x2 = xbuf[...].astype(F32).reshape(slots, dim).astype(BF16)
    m2 = meta_x[...]
    b2 = m2[:, 0:1] - first
    w_half = w_ref[pl.ds(pl.multiple_of(core * half, half), half), :]
    sl2 = slope128(x2, w_half, b2, m2[:, 1:2], hblk)
    dw = dw + mm(spread(sl2, b2, hblk), x2, 0, 0)
    dwbuf[...] = dw.astype(BF16).reshape(chips, piece, dim)
    for t in range(1, chips):
        to = lax.rem(chip + t, chips)
        remote(dwbuf.at[to], dwrecv.at[chip], s3, r3, (2 * to + core, me)).start()
    dwrecv[pl.ds(chip, 1)] = dwbuf[pl.ds(chip, 1)]

    def to_home(s):
        return remote(fsend.at[s], fback.at[s], sb.at[s], rb.at[s], (p, srcs[s]))

    for s in range(2):
        bulk(rrbuf.at[s, pl.ds(0, N_RELAY - 1)], rr.at[s]).wait_recv()
        terms = rrbuf[s].astype(F32).reshape(width, dim).astype(BF16)
        fsend[s] = mm(prel[s * width:(s + 1) * width], terms, 0, 0).astype(BF16)
        to_home(s).start()

    bulk(dwrecv.at[pl.ds(0, chips - 1)], r3).wait_recv()
    total = dwrecv[0].astype(F32)
    for j in range(1, chips):
        total = total + dwrecv[j].astype(F32)
    done = (total / n_pb).astype(BF16)
    fin[...] = done

    def rows_of(c_, j):
        return pl.ds(pl.multiple_of(c_ * half + j * piece, piece), piece)

    wg_ref[rows_of(core, chip), :] = done

    def share(to, j):
        return remote(fin, wg_ref.at[rows_of(core, j)], s4, r4.at[j], (2 * to + core, me))

    for t in range(1, chips):
        share(lax.rem(chip + t, chips), chip).start()
    remote(fin, wg_ref.at[rows_of(core, chip)], s5, r5, (partner, me)).start()

    bulk(nbuf.at[pl.ds(0, N_NEAR - 1)], rn).wait_recv()
    terms = nbuf[...].astype(F32).reshape(width, dim).astype(BF16)
    home_sum = mm(pown[...], terms, 0, 0)
    for s in range(2):
        to_home(s).wait_recv()
        home_sum = home_sum + fback[s].astype(F32)
    dq_ref[...] = home_sum

    for t in range(1, chips):
        other = lax.rem(chip + t, chips)
        share(other, other).wait_recv()
        there = wg_ref.at[rows_of(core, other)]
        remote(there, there, s5, r5, (partner, me)).start()
    bulk(wg_ref.at[pl.ds(pl.multiple_of((1 - core) * half, half), half)], r5).wait_recv()

    bulk(sbuf.at[pl.ds(0, N_NEAR - 1)], s1.at[0]).wait_send()
    for s in range(2):
        chunk_out(s).wait_send()
        bulk(relbuf.at[s, pl.ds(0, N_RELAY - 1)], sr.at[s]).wait_send()
        to_home(s).wait_send()
    fwd_meta.wait_send()
    fwd_rows.wait_send()
    bulk(sbuf2.at[pl.ds(0, n_in)], s2).wait_send()
    bulk(dwbuf.at[pl.ds(0, chips - 1)], s3).wait_send()
    bulk(dwbuf.at[pl.ds(0, chips - 1)], s4).wait_send()
    bulk(wg_ref.at[pl.ds(pl.multiple_of(core * half, half), half)], s5).wait_send()


def write_out(a_ref, b_ref, oa_ref, ob_ref, sems):
    first = pltpu.make_async_copy(b_ref, ob_ref, sems.at[0])
    second = pltpu.make_async_copy(a_ref, oa_ref, sems.at[1])
    first.start()
    second.start()
    first.wait()
    second.wait()


def shards(n_pb, n_lab, queries, label_weights, sibling_blocks, positive_slot):
    rows, dim = queries.shape
    labels = label_weights.shape[0]
    kk = sibling_blocks.shape[1]
    cap = rows * kk // n_lab
    slots = n_lab * cap
    chips = n_pb // 2
    piece = labels // 2 // chips
    width = LIST * cap
    sib = sibling_blocks.T
    pos = positive_slot.reshape(1, -1)
    vmem = pl.BlockSpec(memory_space=pltpu.VMEM)
    hbm = pl.BlockSpec(memory_space=pl.ANY)
    dma = pltpu.SemaphoreType.DMA

    def buf(*lead):
        return pltpu.VMEM((*lead, dim), BF16)

    dq, wg = pl.pallas_call(
        functools.partial(kernel, n_pb, n_lab),
        out_shape=(pltpu.VMEM((rows, dim), F32), pltpu.VMEM((labels, dim), BF16)),
        in_specs=[vmem, hbm, vmem, vmem],
        out_specs=(vmem, vmem),
        scratch_shapes=[
            buf(labels), buf(LIST, cap), buf(2, rows), buf(2, LIST, cap), buf(n_lab, cap), buf(n_lab, cap),
            pltpu.VMEM((width, rows), BF16), pltpu.VMEM((2 * width, rows), BF16),
            pltpu.VMEM((slots, BLOCK), F32), pltpu.VMEM((slots, BLOCK), F32),
            buf(n_lab, cap), buf(LIST, cap), buf(2, LIST, cap), buf(2, rows), buf(2, rows),
            buf(chips, piece), buf(chips, piece), buf(piece),
            dma, dma((1,)), dma, dma((2,)), dma((2,)), dma((2,)), dma((2,)), dma((2,)), dma, dma, dma((2,)), dma((2,)), dma((2,)),
            dma, dma, dma, dma((chips,)), dma, dma,
        ],
        compiler_params=pltpu.CompilerParams(collective_id=0, has_side_effects=True),
    )(queries, label_weights, sib, pos)
    near = functools.partial(pltpu.with_memory_space_constraint, memory_space=pltpu.VMEM)
    return pl.pallas_call(
        write_out,
        out_shape=(jax.ShapeDtypeStruct((rows, dim), F32), jax.ShapeDtypeStruct((labels, dim), BF16)),
        in_specs=[vmem, vmem],
        out_specs=(hbm, hbm),
        scratch_shapes=[dma((2,))],
    )(near(dq), near(wg))


def solution(mesh):
    in_specs = (P(("pb", "lab"), None), P("lab", None), P("pb", None), P("pb"))
    out_specs = (P(("pb", "lab"), None), P("lab", None))
    body = functools.partial(shards, mesh.shape["pb"], mesh.shape["lab"])
    return jax.shard_map(body, mesh=mesh, in_specs=in_specs, out_specs=out_specs, check_vma=False)
```

```python
import functools

import jax
import jax.numpy as jnp
from jax import lax
from jax.experimental import pallas as pl
from jax.experimental.pallas import tpu as pltpu
from jax.sharding import PartitionSpec as P

MESH = pl.DeviceIdType.MESH
BLOCK = 128
HOP = 4
LIST = 16
PARTS = 2
F32 = jnp.float32
BF16 = jnp.bfloat16
SELF_NEAR = 2 * (HOP - 1)
N_NEAR = 2 * (2 * HOP - 1)
N_RELAY = 2 * HOP + 1


def mm(a, b, ca=1, cb=0):
    return lax.dot_general(a, b, (((ca,), (cb,)), ((), ())), preferred_element_type=F32)


def iota(shape, ax):
    return lax.broadcasted_iota(jnp.int32, shape, ax)


def kernel(n_pb, n_lab, q_ref, w_hbm, sib_ref, pos_ref, dq_ref, wg_ref, w_ref, sbuf, fbuf, relbuf, rbuf, xall, sall, slb, pown, prel, meta, meta_x,
           sbuf2, nbuf, rrbuf, fsend, fback, dwbuf, dwrecv, fin,
           sw, s1, rnear, rfar, sf, rf, sr, sx, rx, s2, rn, rr, sb, rb, s3, r3, s4, r4, s5, r5):
    kk, total_rows = sib_ref.shape
    rows, dim = q_ref.shape
    cap = rows * kk // n_lab
    slots = n_lab * cap
    labels = w_hbm.shape[0]
    nblk = labels // BLOCK
    half = labels // 2
    chips = n_pb // 2
    part = half // PARTS
    piece = part // chips
    nz = n_lab // 2
    p = lax.axis_index("pb")
    me = lax.axis_index("lab")
    core = lax.rem(p, 2)
    chip = lax.div(p, 2)
    partner = p + 1 - 2 * core
    my_y = lax.div(me, nz)
    my_z = lax.rem(me, nz)

    def at(dy, dz):
        return lax.rem(my_y + dy, 2) * nz + lax.rem(my_z + dz + nz, nz)

    load_w = pltpu.make_async_copy(w_hbm, w_ref, sw)
    load_w.start()

    barrier = pltpu.get_barrier_semaphore()
    for dz in range(-HOP, HOP + 1):
        for dy in range(2):
            if dz or dy:
                pl.semaphore_signal(barrier, inc=1, device_id=(p, at(dy, dz)), device_id_type=MESH)
    pl.semaphore_signal(barrier, inc=1, device_id=(partner, me), device_id_type=MESH)
    for t in range(1, chips):
        pl.semaphore_signal(barrier, inc=1, device_id=(2 * lax.rem(chip + t, chips) + core, me), device_id_type=MESH)

    src_a, src_b = at(0, -HOP), at(0, HOP)
    upper = (iota((rows, rows), 0) <= iota((rows, rows), 1)).astype(BF16)

    def pick(hit_b, expand):
        want = (lax.rem(iota((expand.shape[0], rows), 0), cap) + 1).astype(F32)
        rank = mm(hit_b, upper)
        on = mm(expand, hit_b)
        return jnp.logical_and(on > 0.5, mm(expand, rank.astype(BF16)) == want)

    sib = sib_ref[...]
    col = iota((total_rows, 3 * rows), 1)
    run_of = jnp.where(col < rows, me, jnp.where(col < 2 * rows, src_a, src_b))
    take = (iota((total_rows, 3 * rows), 0) == run_of * rows + lax.rem(col, rows)).astype(BF16)
    mine3 = mm(sib.astype(BF16), take)

    jrow = iota((LIST, rows), 0)
    jy = lax.rem(jrow, 2)
    jm = lax.div(jrow, 2)

    def lab_of(dy, dz):
        return lax.rem(my_y + dy, 2) * nz + lax.rem(my_z + dz + nz, nz)

    near_ids = jnp.where(jrow < N_NEAR, lab_of(jy, jm - (HOP - 1)), -1)
    ids_a = jnp.where(jrow < N_RELAY, lab_of(jy, jm), -1)
    ids_b = jnp.where(jrow < N_RELAY, lab_of(jnp.where(jrow == N_RELAY - 1, 1, jy), -jm), -1)
    hits = []
    for n, ids in enumerate((near_ids, ids_a, ids_b)):
        hit = jnp.zeros((LIST, rows), F32)
        for k in range(kk):
            blocks = mine3[k:k + 1, n * rows:(n + 1) * rows].astype(jnp.int32)
            hit = jnp.where(jnp.right_shift(blocks, 3) == ids, 1.0, hit)
        hits.append(hit)
    lists = 3 * LIST
    sel3 = pick(jnp.concatenate(hits, axis=0).astype(BF16), (iota((lists * cap, lists), 0) // cap == iota((lists * cap, lists), 1)).astype(BF16))
    sel3 = jnp.where(sel3, 1.0, 0.0).astype(BF16)
    width = LIST * cap
    pown[...] = sel3[:width]
    prel[...] = sel3[width:]
    sbuf[...] = mm(sel3[:width], q_ref[...]).reshape(LIST, cap, dim).astype(BF16)

    pl.semaphore_wait(barrier, 2 * (2 * HOP + 1) - 1 + chips)

    def remote(src, dst, send, recv, dev):
        return pltpu.make_async_remote_copy(
            src_ref=src, dst_ref=dst, send_sem=send, recv_sem=recv, device_id=dev, device_id_type=MESH)

    def chunk_out(s):
        return remote(q_ref, fbuf.at[s], sf.at[s], rf.at[s], (p, at(0, HOP if s == 0 else -HOP)))

    chunk_out(0).start()
    chunk_out(1).start()
    near = [(dz * sg, dy) for dz in range(HOP - 1, -1, -1) for sg in ((1, -1) if dz else (1,)) for dy in (0, 1) if dz or dy]
    for dz, dy in near:
        j = 2 * (dz + HOP - 1) + dy
        remote(sbuf.at[j], rbuf.at[2 * (HOP - 1 - dz) + dy], s1.at[0], rnear, (p, at(dy, dz))).start()
    rbuf[SELF_NEAR:SELF_NEAR + 1] = sbuf[SELF_NEAR:SELF_NEAR + 1]

    qrow = iota((n_lab, total_rows), 1)
    in_run = jnp.right_shift(qrow, 5) == iota((n_lab, total_rows), 0)
    fold = (jnp.bitwise_and(iota((total_rows, rows), 0), rows - 1) == iota((total_rows, rows), 1)).astype(BF16)
    here = jnp.right_shift(sib, 3) == me
    pos = pos_ref[...]
    blk1 = jnp.sum(jnp.where(here, jnp.bitwise_and(sib, 7) + 1, 0), axis=0, keepdims=True)
    is_pos = jnp.logical_and(here, iota((kk, total_rows), 0) == jnp.right_shift(pos, 7))
    col1 = jnp.sum(jnp.where(is_pos, jnp.bitwise_and(pos, BLOCK - 1) + 1, 0), axis=0, keepdims=True)
    packed = jnp.concatenate([jnp.where(in_run, blk1, 0), jnp.where(in_run, col1, 0)], axis=0)
    table = mm(packed.astype(F32).astype(BF16), fold)
    blk_t, col_t = table[:n_lab], table[n_lab:]
    slot = jnp.right_shift(iota((slots, n_lab), 0), 3)
    jj_of = jnp.where(slot < LIST + N_RELAY - 1, slot - (LIST - 1), slot - (LIST + N_RELAY - 2))
    far_a = lab_of(jnp.bitwise_and(jj_of, 1), -HOP - jnp.right_shift(jj_of, 1))
    far_b = lab_of(jnp.where(jj_of == N_RELAY - 1, 1, jnp.bitwise_and(jj_of, 1)), HOP + jnp.right_shift(jj_of, 1))
    source = jnp.where(slot < LIST + N_RELAY - 1, far_a, far_b)
    source = jnp.where(slot == N_NEAR, src_a, jnp.where(slot == N_NEAR + 1, src_b, source))
    source = jnp.where(slot < N_NEAR, lab_of(jnp.bitwise_and(slot, 1), jnp.right_shift(slot, 1) - (HOP - 1)), source)
    expand = (source == iota((slots, n_lab), 1)).astype(BF16)
    sel_lab = pick(jnp.where(blk_t > 0.5, 1.0, 0.0).astype(BF16), expand)
    blk_s = jnp.sum(jnp.where(sel_lab, mm(expand, blk_t.astype(BF16)), 0.0), axis=1, keepdims=True) - 1.0
    pc_s = jnp.sum(jnp.where(sel_lab, mm(expand, col_t.astype(BF16)), 0.0), axis=1, keepdims=True) - 1.0
    lane = iota((slots, BLOCK), 1)
    meta[...] = jnp.where(lane == 0, blk_s, pc_s)
    fwd_meta = remote(meta, meta_x, sx.at[0], rx.at[0], (partner, me))
    fwd_meta.start()
    nbuf[N_NEAR:] = jnp.zeros((LIST - N_NEAR, cap, dim), BF16)
    rrbuf[0, N_RELAY:] = jnp.zeros((LIST - N_RELAY, cap, dim), BF16)
    rrbuf[1, N_RELAY:] = jnp.zeros((LIST - N_RELAY, cap, dim), BF16)

    def stop(s, jj):
        if jj == N_RELAY - 1:
            return (0, HOP) if s == 0 else (1, -HOP)
        m, dy = divmod(jj, 2)
        return dy, (m if s == 0 else -m)

    def far_slot(s, jj):
        return LIST + s * (N_RELAY - 1) + jj - 1

    srcs = (src_a, src_b)
    for s in range(2):
        chunk_out(s).wait_recv()
        out = mm(prel[s * width:(s + 1) * width], fbuf[s])
        relbuf[s] = out.reshape(LIST, cap, dim).astype(BF16)
        for jj in range(N_RELAY - 1, 0, -1):
            dy, dz = stop(s, jj)
            remote(relbuf.at[s, jj], rbuf.at[far_slot(s, jj)], sr.at[s], rfar, (p, at(dy, dz))).start()
        rbuf[N_NEAR + s:N_NEAR + s + 1] = relbuf[s, 0:1]

    def bulk(ref, sem):
        return remote(ref, ref, sem, sem, (partner, me))

    hrows = slots // 2
    hblk = nblk // 2
    first = core.astype(F32) * hblk
    lane_f = iota((hrows, BLOCK), 1).astype(F32)

    def slope128(x, w, b_of, pc, n):
        scores = mm(x, w, 1, 1)
        acc = jnp.zeros((hrows, BLOCK), F32)
        for b in range(n):
            acc = jnp.where(b_of == float(b), scores[:, b * BLOCK:(b + 1) * BLOCK], acc)
        return jax.nn.sigmoid(acc) - jnp.where(lane_f == pc, 1.0, 0.0)

    def spread(sl, b_of, n):
        return jnp.concatenate([jnp.where(b_of == float(b), sl, 0.0) for b in range(n)], axis=1).astype(BF16)

    def fwd_rows(hf):
        return remote(xall.at[pl.ds(hf * hrows, hrows)], xall.at[pl.ds(slots + hf * hrows, hrows)], sx.at[1 + hf], rx.at[1 + hf], (partner, me))

    def own_rows(hf):
        x = rbuf[hf * LIST:(hf + 1) * LIST].astype(F32).reshape(hrows, dim).astype(BF16)
        xall[hf * hrows:(hf + 1) * hrows] = x
        fwd_rows(hf).start()
        b_of = meta[hf * hrows:(hf + 1) * hrows, 0:1]
        sl = slope128(x, w_ref[...], b_of, meta[hf * hrows:(hf + 1) * hrows, 1:2], nblk)
        slb[hf] = sl
        sall[hf * hrows:(hf + 1) * hrows] = spread(sl, b_of - first, hblk)

    def query_terms(hf):
        dq_part = mm(spread(slb[hf], meta[hf * hrows:(hf + 1) * hrows, 0:1], nblk), w_ref[...])
        sbuf2[hf * LIST:(hf + 1) * LIST] = dq_part.reshape(LIST, cap, dim).astype(BF16)

    def partner_rows(hf):
        at_row = slots + hf * hrows
        fwd_rows(hf).wait_recv()
        x = xall[at_row:at_row + hrows]
        b_of = meta_x[hf * hrows:(hf + 1) * hrows, 0:1] - first
        w_half = w_ref[pl.ds(pl.multiple_of(core * half, half), half), :]
        sl = slope128(x, w_half, b_of, meta_x[hf * hrows:(hf + 1) * hrows, 1:2], hblk)
        sall[at_row:at_row + hrows] = spread(sl, b_of, hblk)

    load_w.wait()
    bulk(rbuf.at[pl.ds(0, N_NEAR - 1)], rnear).wait_recv()
    own_rows(0)
    fwd_meta.wait_recv()
    partner_rows(0)
    query_terms(0)
    bulk(rbuf.at[pl.ds(LIST, LIST)], rfar).wait_recv()
    for dz, dy in near:
        remote(sbuf2.at[2 * (dz + HOP - 1) + dy], nbuf.at[2 * (HOP - 1 - dz) + dy], s2, rn, (p, at(dy, dz))).start()
    nbuf[SELF_NEAR:SELF_NEAR + 1] = sbuf2[SELF_NEAR:SELF_NEAR + 1]
    own_rows(1)
    query_terms(1)
    for s in range(2):
        for jj in range(N_RELAY - 1, 0, -1):
            dy, dz = stop(s, jj)
            remote(sbuf2.at[far_slot(s, jj)], rrbuf.at[s, jj], s2, rr.at[s], (p, at(dy, -dz))).start()
        rrbuf[s, 0:1] = sbuf2[N_NEAR + s:N_NEAR + s + 1]
    partner_rows(1)

    nx = chips // 2
    chip_h, chip_x = lax.div(chip, nx), lax.rem(chip, nx)

    def chip_at(dh, dx):
        return lax.rem(chip_h + dh, 2) * nx + lax.rem(chip_x + dx + nx, nx)

    others = [(1, dx) for dx in range(nx - 1, -1, -1)] + [(0, dx) for dx in range(nx - 1, 0, -1)]
    for g in range(PARTS):
        dw = mm(sall[:, g * part:(g + 1) * part], xall[...], 0, 0)
        dwbuf[g] = dw.astype(BF16).reshape(chips, piece, dim)
        for dh, dx in others:
            to = chip_at(dh, dx)
            remote(dwbuf.at[g, to], dwrecv.at[g, chip], s3.at[g], r3.at[g], (2 * to + core, me)).start()
        dwrecv[g, pl.ds(chip, 1)] = dwbuf[g, pl.ds(chip, 1)]

    def to_home(s):
        return remote(fsend.at[s], fback.at[s], sb.at[s], rb.at[s], (p, srcs[s]))

    for s in range(2):
        bulk(rrbuf.at[s, pl.ds(0, N_RELAY - 1)], rr.at[s]).wait_recv()
        terms = rrbuf[s].astype(F32).reshape(width, dim).astype(BF16)
        fsend[s] = mm(prel[s * width:(s + 1) * width], terms, 0, 0).astype(BF16)
        to_home(s).start()

    def rows_of(c_, g, j):
        return pl.ds(pl.multiple_of(c_ * half + g * part + j * piece, piece), piece)

    def share(g, to, j):
        return remote(fin.at[g], wg_ref.at[rows_of(core, g, j)], s4.at[g], r4.at[g, j], (2 * to + core, me))

    ring = nx > 2
    direct = [(1, 0)] + ([(0, 2), (0, 1), (0, -1)] if ring else [(0, dx) for dx in range(1, nx)])
    passed = {(1, 0): [(0, 1), (0, -1)] if ring else [(0, dx) for dx in range(1, nx)], (0, 2): [(1, 0)]}
    second = [(1, 1), (1, -1), (1, 2)] if ring else [(1, dx) for dx in range(1, nx)]

    for g in range(PARTS):
        bulk(dwrecv.at[g, pl.ds(0, chips - 1)], r3.at[g]).wait_recv()
        total = dwrecv[g, 0].astype(F32)
        for j in range(1, chips):
            total = total + dwrecv[g, j].astype(F32)
        done = (total / n_pb).astype(BF16)
        fin[g] = done
        wg_ref[rows_of(core, g, chip), :] = done
        for dh, dx in direct:
            share(g, chip_at(dh, dx), chip).start()
        remote(fin.at[g], wg_ref.at[rows_of(core, g, chip)], s5, r5, (partner, me)).start()

    def query_home():
        bulk(nbuf.at[pl.ds(0, N_NEAR - 1)], rn).wait_recv()
        terms = nbuf[...].astype(F32).reshape(width, dim).astype(BF16)
        home_sum = mm(pown[...], terms, 0, 0)
        for s in range(2):
            to_home(s).wait_recv()
            home_sum = home_sum + fback[s].astype(F32)
        dq_ref[...] = home_sum

    def arrived(g, dh, dx):
        owner = chip_at(dh, dx)
        share(g, owner, owner).wait_recv()
        there = wg_ref.at[rows_of(core, g, owner)]
        for fh, fx in passed.get((dh, dx), []):
            remote(there, there, s4.at[g], r4.at[g, owner], (2 * chip_at(fh, fx) + core, me)).start()
        remote(there, there, s5, r5, (partner, me)).start()

    for g in range(PARTS):
        for dh, dx in direct:
            arrived(g, dh, dx)
    query_home()
    for g in range(PARTS):
        for dh, dx in second:
            arrived(g, dh, dx)
    bulk(wg_ref.at[pl.ds(pl.multiple_of((1 - core) * half, half), half)], r5).wait_recv()

    bulk(sbuf.at[pl.ds(0, N_NEAR - 1)], s1.at[0]).wait_send()
    for s in range(2):
        chunk_out(s).wait_send()
        bulk(relbuf.at[s, pl.ds(0, N_RELAY - 1)], sr.at[s]).wait_send()
        to_home(s).wait_send()
        fwd_rows(s).wait_send()
    fwd_meta.wait_send()
    bulk(sbuf2.at[pl.ds(0, n_lab - 3)], s2).wait_send()
    for g in range(PARTS):
        bulk(dwbuf.at[g, pl.ds(0, chips - 1)], s3.at[g]).wait_send()
        bulk(dwbuf.at[g, pl.ds(0, chips - 1)], s4.at[g]).wait_send()
    bulk(wg_ref.at[pl.ds(pl.multiple_of(core * half, half), half)], s5).wait_send()


def write_out(a_ref, b_ref, oa_ref, ob_ref, sems):
    first = pltpu.make_async_copy(b_ref, ob_ref, sems.at[0])
    second = pltpu.make_async_copy(a_ref, oa_ref, sems.at[1])
    first.start()
    second.start()
    first.wait()
    second.wait()


def shards(n_pb, n_lab, queries, label_weights, sibling_blocks, positive_slot):
    rows, dim = queries.shape
    labels = label_weights.shape[0]
    kk = sibling_blocks.shape[1]
    cap = rows * kk // n_lab
    slots = n_lab * cap
    chips = n_pb // 2
    piece = labels // 2 // PARTS // chips
    width = LIST * cap
    sib = sibling_blocks.T
    pos = positive_slot.reshape(1, -1)
    vmem = pl.BlockSpec(memory_space=pltpu.VMEM)
    hbm = pl.BlockSpec(memory_space=pl.ANY)
    dma = pltpu.SemaphoreType.DMA

    def buf(*lead):
        return pltpu.VMEM((*lead, dim), BF16)

    dq, wg = pl.pallas_call(
        functools.partial(kernel, n_pb, n_lab),
        out_shape=(pltpu.VMEM((rows, dim), F32), pltpu.VMEM((labels, dim), BF16)),
        in_specs=[vmem, hbm, vmem, vmem],
        out_specs=(vmem, vmem),
        scratch_shapes=[
            buf(labels), buf(LIST, cap), buf(2, rows), buf(2, LIST, cap), buf(n_lab, cap), buf(2 * slots),
            pltpu.VMEM((2 * slots, labels // 2), BF16), pltpu.VMEM((2, slots // 2, BLOCK), F32),
            pltpu.VMEM((width, rows), BF16), pltpu.VMEM((2 * width, rows), BF16),
            pltpu.VMEM((slots, BLOCK), F32), pltpu.VMEM((slots, BLOCK), F32),
            buf(n_lab, cap), buf(LIST, cap), buf(2, LIST, cap), buf(2, rows), buf(2, rows),
            buf(PARTS, chips, piece), buf(PARTS, chips, piece), buf(PARTS, piece),
            dma, dma((1,)), dma, dma, dma((2,)), dma((2,)), dma((2,)), dma((3,)), dma((3,)), dma, dma, dma((2,)), dma((2,)), dma((2,)),
            dma((PARTS,)), dma((PARTS,)), dma((PARTS,)), dma((PARTS, chips)), dma, dma,
        ],
        compiler_params=pltpu.CompilerParams(collective_id=0, has_side_effects=True),
    )(queries, label_weights, sib, pos)
    near = functools.partial(pltpu.with_memory_space_constraint, memory_space=pltpu.VMEM)
    return pl.pallas_call(
        write_out,
        out_shape=(jax.ShapeDtypeStruct((rows, dim), F32), jax.ShapeDtypeStruct((labels, dim), BF16)),
        in_specs=[vmem, vmem],
        out_specs=(hbm, hbm),
        scratch_shapes=[dma((2,))],
    )(near(dq), near(wg))


def solution(mesh):
    in_specs = (P(("pb", "lab"), None), P("lab", None), P("pb", None), P("pb"))
    out_specs = (P(("pb", "lab"), None), P("lab", None))
    body = functools.partial(shards, mesh.shape["pb"], mesh.shape["lab"])
    return jax.shard_map(body, mesh=mesh, in_specs=in_specs, out_specs=out_specs, check_vma=False)
```

```python
import functools

import jax
import jax.numpy as jnp
from jax import lax
from jax.experimental import pallas as pl
from jax.experimental.pallas import tpu as pltpu
from jax.sharding import PartitionSpec as P

MESH = pl.DeviceIdType.MESH
BLOCK = 128
HOP = 4
LIST = 16
PARTS = 2
F32 = jnp.float32
BF16 = jnp.bfloat16
SELF_NEAR = 2 * (HOP - 1)
N_NEAR = 2 * (2 * HOP - 1)
N_RELAY = 2 * HOP + 1


def mm(a, b, ca=1, cb=0):
    return lax.dot_general(a, b, (((ca,), (cb,)), ((), ())), preferred_element_type=F32)


def iota(shape, ax):
    return lax.broadcasted_iota(jnp.int32, shape, ax)


def kernel(n_pb, n_lab, q_hbm, w_hbm, sib_hbm, pos_hbm, dq_ref, wg_ref, q_ref, sib_ref, pos_ref, w_ref, sbuf, fbuf, relbuf, rbuf, xall, sall, slb, pown, prel, meta, meta_x,
           sbuf2, nbuf, rrbuf, fsend, fback, dwbuf, dwrecv, comb, fin,
           sq, sw, s1, rnear, rfar, sf, rf, sr, sx, rx, s2, rn, rr, sb, rb, s3, r3, s4, r4, s5, r5, r6):
    kk, total_rows = sib_hbm.shape
    rows, dim = q_hbm.shape
    cap = rows * kk // n_lab
    slots = n_lab * cap
    labels = w_hbm.shape[0]
    nblk = labels // BLOCK
    half = labels // 2
    chips = n_pb // 2
    part = half // PARTS
    piece = part // chips
    nz = n_lab // 2
    p = lax.axis_index("pb")
    me = lax.axis_index("lab")
    core = lax.rem(p, 2)
    chip = lax.div(p, 2)
    partner = p + 1 - 2 * core
    my_y = lax.div(me, nz)
    my_z = lax.rem(me, nz)

    def at(dy, dz):
        return lax.rem(my_y + dy, 2) * nz + lax.rem(my_z + dz + nz, nz)

    loads = [
        pltpu.make_async_copy(src, dst, sq.at[n])
        for n, (src, dst) in enumerate(((sib_hbm, sib_ref), (q_hbm, q_ref), (pos_hbm, pos_ref)))
    ]
    for load in loads:
        load.start()
    load_w = pltpu.make_async_copy(w_hbm, w_ref, sw)
    load_w.start()

    barrier = pltpu.get_barrier_semaphore()
    for dz in range(-HOP, HOP + 1):
        for dy in range(2):
            if dz or dy:
                pl.semaphore_signal(barrier, inc=1, device_id=(p, at(dy, dz)), device_id_type=MESH)
    pl.semaphore_signal(barrier, inc=1, device_id=(partner, me), device_id_type=MESH)
    for t in range(1, chips):
        pl.semaphore_signal(barrier, inc=1, device_id=(2 * lax.rem(chip + t, chips) + core, me), device_id_type=MESH)

    src_a, src_b = at(0, -HOP), at(0, HOP)
    upper = (iota((rows, rows), 0) <= iota((rows, rows), 1)).astype(BF16)

    def pick(hit_b, expand):
        want = (lax.rem(iota((expand.shape[0], rows), 0), cap) + 1).astype(F32)
        rank = mm(hit_b, upper)
        on = mm(expand, hit_b)
        return jnp.logical_and(on > 0.5, mm(expand, rank.astype(BF16)) == want)

    for load in loads:
        load.wait()
    sib = sib_ref[...]
    col = iota((total_rows, 3 * rows), 1)
    run_of = jnp.where(col < rows, me, jnp.where(col < 2 * rows, src_a, src_b))
    take = (iota((total_rows, 3 * rows), 0) == run_of * rows + lax.rem(col, rows)).astype(BF16)
    mine3 = mm(sib.astype(BF16), take)

    jrow = iota((LIST, rows), 0)
    jy = lax.rem(jrow, 2)
    jm = lax.div(jrow, 2)

    def lab_of(dy, dz):
        return lax.rem(my_y + dy, 2) * nz + lax.rem(my_z + dz + nz, nz)

    near_ids = jnp.where(jrow < N_NEAR, lab_of(jy, jm - (HOP - 1)), -1)
    ids_a = jnp.where(jrow < N_RELAY, lab_of(jy, jm), -1)
    ids_b = jnp.where(jrow < N_RELAY, lab_of(jnp.where(jrow == N_RELAY - 1, 1, jy), -jm), -1)
    hits = []
    for n, ids in enumerate((near_ids, ids_a, ids_b)):
        hit = jnp.zeros((LIST, rows), F32)
        for k in range(kk):
            blocks = mine3[k:k + 1, n * rows:(n + 1) * rows].astype(jnp.int32)
            hit = jnp.where(jnp.right_shift(blocks, 3) == ids, 1.0, hit)
        hits.append(hit)
    lists = 3 * LIST
    sel3 = pick(jnp.concatenate(hits, axis=0).astype(BF16), (iota((lists * cap, lists), 0) // cap == iota((lists * cap, lists), 1)).astype(BF16))
    sel3 = jnp.where(sel3, 1.0, 0.0).astype(BF16)
    width = LIST * cap
    pown[...] = sel3[:width]
    prel[...] = sel3[width:]
    sbuf[...] = mm(sel3[:width], q_ref[...]).reshape(LIST, cap, dim).astype(BF16)

    pl.semaphore_wait(barrier, 2 * (2 * HOP + 1) - 1 + chips)

    def remote(src, dst, send, recv, dev):
        return pltpu.make_async_remote_copy(
            src_ref=src, dst_ref=dst, send_sem=send, recv_sem=recv, device_id=dev, device_id_type=MESH)

    def chunk_out(s):
        return remote(q_ref, fbuf.at[s], sf.at[s], rf.at[s], (p, at(0, HOP if s == 0 else -HOP)))

    chunk_out(0).start()
    chunk_out(1).start()
    near = [(dz * sg, dy) for dz in range(HOP - 1, -1, -1) for sg in ((1, -1) if dz else (1,)) for dy in (0, 1) if dz or dy]
    for dz, dy in near:
        j = 2 * (dz + HOP - 1) + dy
        remote(sbuf.at[j], rbuf.at[2 * (HOP - 1 - dz) + dy], s1.at[0], rnear, (p, at(dy, dz))).start()
    rbuf[SELF_NEAR:SELF_NEAR + 1] = sbuf[SELF_NEAR:SELF_NEAR + 1]

    qrow = iota((n_lab, total_rows), 1)
    in_run = jnp.right_shift(qrow, 5) == iota((n_lab, total_rows), 0)
    fold = (jnp.bitwise_and(iota((total_rows, rows), 0), rows - 1) == iota((total_rows, rows), 1)).astype(BF16)
    here = jnp.right_shift(sib, 3) == me
    pos = pos_ref[...]
    blk1 = jnp.sum(jnp.where(here, jnp.bitwise_and(sib, 7) + 1, 0), axis=0, keepdims=True)
    is_pos = jnp.logical_and(here, iota((kk, total_rows), 0) == jnp.right_shift(pos, 7))
    col1 = jnp.sum(jnp.where(is_pos, jnp.bitwise_and(pos, BLOCK - 1) + 1, 0), axis=0, keepdims=True)
    packed = jnp.concatenate([jnp.where(in_run, blk1, 0), jnp.where(in_run, col1, 0)], axis=0)
    table = mm(packed.astype(F32).astype(BF16), fold)
    blk_t, col_t = table[:n_lab], table[n_lab:]
    slot = jnp.right_shift(iota((slots, n_lab), 0), 3)
    jj_of = jnp.where(slot < LIST + N_RELAY - 1, slot - (LIST - 1), slot - (LIST + N_RELAY - 2))
    far_a = lab_of(jnp.bitwise_and(jj_of, 1), -HOP - jnp.right_shift(jj_of, 1))
    far_b = lab_of(jnp.where(jj_of == N_RELAY - 1, 1, jnp.bitwise_and(jj_of, 1)), HOP + jnp.right_shift(jj_of, 1))
    source = jnp.where(slot < LIST + N_RELAY - 1, far_a, far_b)
    source = jnp.where(slot == N_NEAR, src_a, jnp.where(slot == N_NEAR + 1, src_b, source))
    source = jnp.where(slot < N_NEAR, lab_of(jnp.bitwise_and(slot, 1), jnp.right_shift(slot, 1) - (HOP - 1)), source)
    expand = (source == iota((slots, n_lab), 1)).astype(BF16)
    sel_lab = pick(jnp.where(blk_t > 0.5, 1.0, 0.0).astype(BF16), expand)
    blk_s = jnp.sum(jnp.where(sel_lab, mm(expand, blk_t.astype(BF16)), 0.0), axis=1, keepdims=True) - 1.0
    pc_s = jnp.sum(jnp.where(sel_lab, mm(expand, col_t.astype(BF16)), 0.0), axis=1, keepdims=True) - 1.0
    lane = iota((slots, BLOCK), 1)
    meta[...] = jnp.where(lane == 0, blk_s, pc_s)
    fwd_meta = remote(meta, meta_x, sx.at[0], rx.at[0], (partner, me))
    fwd_meta.start()
    nbuf[N_NEAR:] = jnp.zeros((LIST - N_NEAR, cap, dim), BF16)
    rrbuf[0, N_RELAY:] = jnp.zeros((LIST - N_RELAY, cap, dim), BF16)
    rrbuf[1, N_RELAY:] = jnp.zeros((LIST - N_RELAY, cap, dim), BF16)

    def stop(s, jj):
        if jj == N_RELAY - 1:
            return (0, HOP) if s == 0 else (1, -HOP)
        m, dy = divmod(jj, 2)
        return dy, (m if s == 0 else -m)

    def far_slot(s, jj):
        return LIST + s * (N_RELAY - 1) + jj - 1

    srcs = (src_a, src_b)
    for s in range(2):
        chunk_out(s).wait_recv()
        out = mm(prel[s * width:(s + 1) * width], fbuf[s])
        relbuf[s] = out.reshape(LIST, cap, dim).astype(BF16)
        for jj in range(N_RELAY - 1, 0, -1):
            dy, dz = stop(s, jj)
            remote(relbuf.at[s, jj], rbuf.at[far_slot(s, jj)], sr.at[s], rfar, (p, at(dy, dz))).start()
        rbuf[N_NEAR + s:N_NEAR + s + 1] = relbuf[s, 0:1]

    def bulk(ref, sem):
        return remote(ref, ref, sem, sem, (partner, me))

    hrows = slots // 2
    hblk = nblk // 2
    first = core.astype(F32) * hblk
    lane_f = iota((hrows, BLOCK), 1).astype(F32)

    def slope128(x, w, b_of, pc, n):
        scores = mm(x, w, 1, 1)
        acc = jnp.zeros((hrows, BLOCK), F32)
        for b in range(n):
            acc = jnp.where(b_of == float(b), scores[:, b * BLOCK:(b + 1) * BLOCK], acc)
        return jax.nn.sigmoid(acc) - jnp.where(lane_f == pc, 1.0, 0.0)

    def spread(sl, b_of, n):
        return jnp.concatenate([jnp.where(b_of == float(b), sl, 0.0) for b in range(n)], axis=1).astype(BF16)

    def fwd_rows(hf):
        return remote(xall.at[pl.ds(hf * hrows, hrows)], xall.at[pl.ds(slots + hf * hrows, hrows)], sx.at[1 + hf], rx.at[1 + hf], (partner, me))

    def own_rows(hf):
        x = rbuf[hf * LIST:(hf + 1) * LIST].astype(F32).reshape(hrows, dim).astype(BF16)
        xall[hf * hrows:(hf + 1) * hrows] = x
        fwd_rows(hf).start()
        b_of = meta[hf * hrows:(hf + 1) * hrows, 0:1]
        sl = slope128(x, w_ref[...], b_of, meta[hf * hrows:(hf + 1) * hrows, 1:2], nblk)
        slb[hf] = sl
        sall[hf * hrows:(hf + 1) * hrows] = spread(sl, b_of - first, hblk)

    def query_terms(hf):
        dq_part = mm(spread(slb[hf], meta[hf * hrows:(hf + 1) * hrows, 0:1], nblk), w_ref[...])
        sbuf2[hf * LIST:(hf + 1) * LIST] = dq_part.reshape(LIST, cap, dim).astype(BF16)

    def partner_rows(hf):
        at_row = slots + hf * hrows
        fwd_rows(hf).wait_recv()
        x = xall[at_row:at_row + hrows]
        b_of = meta_x[hf * hrows:(hf + 1) * hrows, 0:1] - first
        w_half = w_ref[pl.ds(pl.multiple_of(core * half, half), half), :]
        sl = slope128(x, w_half, b_of, meta_x[hf * hrows:(hf + 1) * hrows, 1:2], hblk)
        sall[at_row:at_row + hrows] = spread(sl, b_of, hblk)

    load_w.wait()
    bulk(rbuf.at[pl.ds(0, N_NEAR - 1)], rnear).wait_recv()
    own_rows(0)
    fwd_meta.wait_recv()
    partner_rows(0)
    query_terms(0)
    bulk(rbuf.at[pl.ds(LIST, LIST)], rfar).wait_recv()
    for dz, dy in near:
        remote(sbuf2.at[2 * (dz + HOP - 1) + dy], nbuf.at[2 * (HOP - 1 - dz) + dy], s2, rn, (p, at(dy, dz))).start()
    nbuf[SELF_NEAR:SELF_NEAR + 1] = sbuf2[SELF_NEAR:SELF_NEAR + 1]
    own_rows(1)
    query_terms(1)
    for s in range(2):
        for jj in range(N_RELAY - 1, 0, -1):
            dy, dz = stop(s, jj)
            remote(sbuf2.at[far_slot(s, jj)], rrbuf.at[s, jj], s2, rr.at[s], (p, at(dy, -dz))).start()
        rrbuf[s, 0:1] = sbuf2[N_NEAR + s:N_NEAR + s + 1]
    partner_rows(1)

    nx = chips // 2
    chip_h, chip_x = lax.div(chip, nx), lax.rem(chip, nx)

    def chip_at(dh, dx):
        return lax.rem(chip_h + dh, 2) * nx + lax.rem(chip_x + dx + nx, nx)

    ring = nx > 2
    others = [(1, 1), (1, -1), (0, 2), (0, 1), (0, -1)] if ring else [(1, dx) for dx in range(nx)] + [(0, dx) for dx in range(1, nx)]
    across = chip_at(1, 0)

    def to_across(g):
        return remote(dwbuf.at[g, across], dwrecv.at[g, chip], s3.at[g], r3.at[g], (2 * across + core, me))

    def corner(g):
        return remote(dwbuf.at[g, chip_at(1, 2)], comb.at[g], s3.at[g], r6.at[g], (2 * chip_at(0, 2) + core, me))

    for g in range(PARTS):
        dw = mm(sall[:, g * part:(g + 1) * part], xall[...], 0, 0)
        dwbuf[g] = dw.astype(BF16).reshape(chips, piece, dim)
        if ring:
            corner(g).start()
        for dh, dx in others:
            to = chip_at(dh, dx)
            remote(dwbuf.at[g, to], dwrecv.at[g, chip], s3.at[g], r3.at[g], (2 * to + core, me)).start()
        dwrecv[g, pl.ds(chip, 1)] = dwbuf[g, pl.ds(chip, 1)]

    if ring:
        for g in range(PARTS):
            corner(g).wait_recv()
            both = dwbuf[g, pl.ds(across, 1)].astype(F32) + comb[g:g + 1].astype(F32)
            dwbuf[g, pl.ds(across, 1)] = both.astype(BF16)
            to_across(g).start()

    def to_home(s):
        return remote(fsend.at[s], fback.at[s], sb.at[s], rb.at[s], (p, srcs[s]))

    def rows_of(c_, g, j):
        return pl.ds(pl.multiple_of(c_ * half + g * part + j * piece, piece), piece)

    def share(g, to, j):
        return remote(fin.at[g], wg_ref.at[rows_of(core, g, j)], s4.at[g], r4.at[g, j], (2 * to + core, me))

    direct = [(1, 0)] + ([(0, 2), (0, 1), (0, -1)] if ring else [(0, dx) for dx in range(1, nx)])
    passed = {(1, 0): [(0, 1), (0, -1)] if ring else [(0, dx) for dx in range(1, nx)], (0, 2): [(1, 0)]}
    second = [(1, 1), (1, -1), (1, 2)] if ring else [(1, dx) for dx in range(1, nx)]

    for g in range(PARTS):
        came = others + ([(1, 0)] if ring else [])
        bulk(dwrecv.at[g, pl.ds(0, len(came))], r3.at[g]).wait_recv()
        total = dwrecv[g, pl.ds(chip, 1)].astype(F32)
        for dh, dx in came:
            total = total + dwrecv[g, pl.ds(chip_at(dh, dx), 1)].astype(F32)
        done = (total[0] / n_pb).astype(BF16)
        fin[g] = done
        wg_ref[rows_of(core, g, chip), :] = done
        for dh, dx in direct:
            share(g, chip_at(dh, dx), chip).start()
        remote(fin.at[g], wg_ref.at[rows_of(core, g, chip)], s5, r5, (partner, me)).start()
        if g == 0:
            for s in range(2):
                bulk(rrbuf.at[s, pl.ds(0, N_RELAY - 1)], rr.at[s]).wait_recv()
                terms = rrbuf[s].astype(F32).reshape(width, dim).astype(BF16)
                fsend[s] = mm(prel[s * width:(s + 1) * width], terms, 0, 0).astype(BF16)
                to_home(s).start()

    def query_home():
        bulk(nbuf.at[pl.ds(0, N_NEAR - 1)], rn).wait_recv()
        terms = nbuf[...].astype(F32).reshape(width, dim).astype(BF16)
        home_sum = mm(pown[...], terms, 0, 0)
        for s in range(2):
            to_home(s).wait_recv()
            home_sum = home_sum + fback[s].astype(F32)
        dq_ref[...] = home_sum

    def arrived(g, dh, dx):
        owner = chip_at(dh, dx)
        share(g, owner, owner).wait_recv()
        there = wg_ref.at[rows_of(core, g, owner)]
        for fh, fx in passed.get((dh, dx), []):
            remote(there, there, s4.at[g], r4.at[g, owner], (2 * chip_at(fh, fx) + core, me)).start()
        remote(there, there, s5, r5, (partner, me)).start()

    for g in range(PARTS):
        for dh, dx in direct:
            arrived(g, dh, dx)
    for g in range(PARTS):
        for dh, dx in second:
            arrived(g, dh, dx)
    query_home()
    bulk(wg_ref.at[pl.ds(pl.multiple_of((1 - core) * half, half), half)], r5).wait_recv()

    bulk(sbuf.at[pl.ds(0, N_NEAR - 1)], s1.at[0]).wait_send()
    for s in range(2):
        chunk_out(s).wait_send()
        bulk(relbuf.at[s, pl.ds(0, N_RELAY - 1)], sr.at[s]).wait_send()
        to_home(s).wait_send()
        fwd_rows(s).wait_send()
    fwd_meta.wait_send()
    bulk(sbuf2.at[pl.ds(0, n_lab - 3)], s2).wait_send()
    for g in range(PARTS):
        bulk(dwbuf.at[g, pl.ds(0, chips - 1)], s3.at[g]).wait_send()
        bulk(dwbuf.at[g, pl.ds(0, chips - 1)], s4.at[g]).wait_send()
    bulk(wg_ref.at[pl.ds(pl.multiple_of(core * half, half), half)], s5).wait_send()


def write_out(a_ref, b_ref, oa_ref, ob_ref, sems):
    first = pltpu.make_async_copy(b_ref, ob_ref, sems.at[0])
    second = pltpu.make_async_copy(a_ref, oa_ref, sems.at[1])
    first.start()
    second.start()
    first.wait()
    second.wait()


def shards(n_pb, n_lab, queries, label_weights, sibling_blocks, positive_slot):
    rows, dim = queries.shape
    labels = label_weights.shape[0]
    kk = sibling_blocks.shape[1]
    cap = rows * kk // n_lab
    slots = n_lab * cap
    chips = n_pb // 2
    piece = labels // 2 // PARTS // chips
    width = LIST * cap
    sib = sibling_blocks.T
    pos = positive_slot.reshape(1, -1)
    vmem = pl.BlockSpec(memory_space=pltpu.VMEM)
    hbm = pl.BlockSpec(memory_space=pl.ANY)
    dma = pltpu.SemaphoreType.DMA

    def buf(*lead):
        return pltpu.VMEM((*lead, dim), BF16)

    dq, wg = pl.pallas_call(
        functools.partial(kernel, n_pb, n_lab),
        out_shape=(pltpu.VMEM((rows, dim), F32), pltpu.VMEM((labels, dim), BF16)),
        in_specs=[hbm] * 4,
        out_specs=(vmem, vmem),
        scratch_shapes=[
            buf(rows), pltpu.VMEM(sib.shape, jnp.int32), pltpu.VMEM(pos.shape, jnp.int32),
            buf(labels), buf(LIST, cap), buf(2, rows), buf(2, LIST, cap), buf(n_lab, cap), buf(2 * slots),
            pltpu.VMEM((2 * slots, labels // 2), BF16), pltpu.VMEM((2, slots // 2, BLOCK), F32),
            pltpu.VMEM((width, rows), BF16), pltpu.VMEM((2 * width, rows), BF16),
            pltpu.VMEM((slots, BLOCK), F32), pltpu.VMEM((slots, BLOCK), F32),
            buf(n_lab, cap), buf(LIST, cap), buf(2, LIST, cap), buf(2, rows), buf(2, rows),
            buf(PARTS, chips, piece), buf(PARTS, chips, piece), buf(PARTS, piece), buf(PARTS, piece),
            dma((3,)), dma, dma((1,)), dma, dma, dma((2,)), dma((2,)), dma((2,)), dma((3,)), dma((3,)), dma, dma, dma((2,)), dma((2,)), dma((2,)),
            dma((PARTS,)), dma((PARTS,)), dma((PARTS,)), dma((PARTS, chips)), dma, dma, dma((PARTS,)),
        ],
        compiler_params=pltpu.CompilerParams(collective_id=0, has_side_effects=True),
    )(queries, label_weights, sib, pos)
    near = functools.partial(pltpu.with_memory_space_constraint, memory_space=pltpu.VMEM)
    return pl.pallas_call(
        write_out,
        out_shape=(jax.ShapeDtypeStruct((rows, dim), F32), jax.ShapeDtypeStruct((labels, dim), BF16)),
        in_specs=[vmem, vmem],
        out_specs=(hbm, hbm),
        scratch_shapes=[dma((2,))],
    )(near(dq), near(wg))


def solution(mesh):
    in_specs = (P(("pb", "lab"), None), P("lab", None), P("pb", None), P("pb"))
    out_specs = (P(("pb", "lab"), None), P("lab", None))
    body = functools.partial(shards, mesh.shape["pb"], mesh.shape["lab"])
    return jax.shard_map(body, mesh=mesh, in_specs=in_specs, out_specs=out_specs, check_vma=False)
```

```python
import functools

import jax
import jax.numpy as jnp
from jax import lax
from jax.experimental import pallas as pl
from jax.experimental.pallas import tpu as pltpu
from jax.sharding import PartitionSpec as P

MESH = pl.DeviceIdType.MESH
BLOCK = 128
HOP = 4
LIST = 16
PARTS = 2
F32 = jnp.float32
BF16 = jnp.bfloat16
SELF_NEAR = 2 * (HOP - 1)
N_NEAR = 2 * (2 * HOP - 1)
N_RELAY = 2 * HOP + 1


def mm(a, b, ca=1, cb=0):
    return lax.dot_general(a, b, (((ca,), (cb,)), ((), ())), preferred_element_type=F32)


def iota(shape, ax):
    return lax.broadcasted_iota(jnp.int32, shape, ax)


def kernel(n_pb, n_lab, q_hbm, w_hbm, sib_hbm, pos_hbm, dq_ref, wg_ref, q_ref, sib_ref, pos_ref, w_ref, sbuf, fbuf, relbuf, rbuf, xall, sall, slb, pown, prel, meta, meta_x,
           sbuf2, nbuf, rrbuf, fsend, fback, dwbuf, dwrecv, comb, fin,
           sq, sw, s1, rnear, rfar, sf, rf, sr, sx, rx, s2, rn, rr, sb, rb, s3, r3, s4, r4, s5, r5, r6):
    kk, total_rows = sib_hbm.shape
    rows, dim = q_hbm.shape
    cap = rows * kk // n_lab
    slots = n_lab * cap
    labels = w_hbm.shape[0]
    nblk = labels // BLOCK
    half = labels // 2
    chips = n_pb // 2
    part = half // PARTS
    piece = part // chips
    nz = n_lab // 2
    p = lax.axis_index("pb")
    me = lax.axis_index("lab")
    core = lax.rem(p, 2)
    chip = lax.div(p, 2)
    partner = p + 1 - 2 * core
    my_y = lax.div(me, nz)
    my_z = lax.rem(me, nz)

    def at(dy, dz):
        return lax.rem(my_y + dy, 2) * nz + lax.rem(my_z + dz + nz, nz)

    loads = [
        pltpu.make_async_copy(src, dst, sq.at[n])
        for n, (src, dst) in enumerate(((sib_hbm, sib_ref), (q_hbm, q_ref), (pos_hbm, pos_ref)))
    ]
    for load in loads:
        load.start()
    load_w = pltpu.make_async_copy(w_hbm, w_ref, sw)
    load_w.start()

    barrier = pltpu.get_barrier_semaphore()
    for dz in sorted(range(-HOP, HOP + 1), key=abs, reverse=True):
        for dy in (1, 0):
            if dz or dy:
                pl.semaphore_signal(barrier, inc=1, device_id=(p, at(dy, dz)), device_id_type=MESH)
    pl.semaphore_signal(barrier, inc=1, device_id=(partner, me), device_id_type=MESH)
    for t in range(1, chips):
        pl.semaphore_signal(barrier, inc=1, device_id=(2 * lax.rem(chip + t, chips) + core, me), device_id_type=MESH)

    src_a, src_b = at(0, -HOP), at(0, HOP)
    upper = (iota((rows, rows), 0) <= iota((rows, rows), 1)).astype(BF16)

    def pick(hit_b, expand):
        want = (lax.rem(iota((expand.shape[0], rows), 0), cap) + 1).astype(F32)
        rank = mm(hit_b, upper)
        on = mm(expand, hit_b)
        return jnp.logical_and(on > 0.5, mm(expand, rank.astype(BF16)) == want)

    for load in loads:
        load.wait()
    sib = sib_ref[...]
    col = iota((total_rows, 3 * rows), 1)
    run_of = jnp.where(col < rows, me, jnp.where(col < 2 * rows, src_a, src_b))
    take = (iota((total_rows, 3 * rows), 0) == run_of * rows + lax.rem(col, rows)).astype(BF16)
    mine3 = mm(sib.astype(BF16), take)

    jrow = iota((LIST, rows), 0)
    jy = lax.rem(jrow, 2)
    jm = lax.div(jrow, 2)

    def lab_of(dy, dz):
        return lax.rem(my_y + dy, 2) * nz + lax.rem(my_z + dz + nz, nz)

    near_ids = jnp.where(jrow < N_NEAR, lab_of(jy, jm - (HOP - 1)), -1)
    ids_a = jnp.where(jrow < N_RELAY, lab_of(jy, jm), -1)
    ids_b = jnp.where(jrow < N_RELAY, lab_of(jnp.where(jrow == N_RELAY - 1, 1, jy), -jm), -1)
    hits = []
    for n, ids in enumerate((near_ids, ids_a, ids_b)):
        hit = jnp.zeros((LIST, rows), F32)
        for k in range(kk):
            blocks = mine3[k:k + 1, n * rows:(n + 1) * rows].astype(jnp.int32)
            hit = jnp.where(jnp.right_shift(blocks, 3) == ids, 1.0, hit)
        hits.append(hit)
    lists = 3 * LIST
    sel3 = pick(jnp.concatenate(hits, axis=0).astype(BF16), (iota((lists * cap, lists), 0) // cap == iota((lists * cap, lists), 1)).astype(BF16))
    sel3 = jnp.where(sel3, 1.0, 0.0).astype(BF16)
    width = LIST * cap
    pown[...] = sel3[:width]
    prel[...] = sel3[width:]
    sbuf[...] = mm(sel3[:width], q_ref[...]).reshape(LIST, cap, dim).astype(BF16)

    pl.semaphore_wait(barrier, 2 * (2 * HOP + 1) - 1 + chips)

    def remote(src, dst, send, recv, dev):
        return pltpu.make_async_remote_copy(
            src_ref=src, dst_ref=dst, send_sem=send, recv_sem=recv, device_id=dev, device_id_type=MESH)

    def chunk_out(s):
        return remote(q_ref, fbuf.at[s], sf.at[s], rf.at[s], (p, at(0, HOP if s == 0 else -HOP)))

    chunk_out(0).start()
    chunk_out(1).start()
    near = [(dz * sg, dy) for dz in range(HOP - 1, -1, -1) for sg in ((1, -1) if dz else (1,)) for dy in (0, 1) if dz or dy]

    qrow = iota((n_lab, total_rows), 1)
    in_run = jnp.right_shift(qrow, 5) == iota((n_lab, total_rows), 0)
    fold = (jnp.bitwise_and(iota((total_rows, rows), 0), rows - 1) == iota((total_rows, rows), 1)).astype(BF16)
    here = jnp.right_shift(sib, 3) == me
    pos = pos_ref[...]
    blk1 = jnp.sum(jnp.where(here, jnp.bitwise_and(sib, 7) + 1, 0), axis=0, keepdims=True)
    is_pos = jnp.logical_and(here, iota((kk, total_rows), 0) == jnp.right_shift(pos, 7))
    col1 = jnp.sum(jnp.where(is_pos, jnp.bitwise_and(pos, BLOCK - 1) + 1, 0), axis=0, keepdims=True)
    packed = jnp.concatenate([jnp.where(in_run, blk1, 0), jnp.where(in_run, col1, 0)], axis=0)
    table = mm(packed.astype(F32).astype(BF16), fold)
    blk_t, col_t = table[:n_lab], table[n_lab:]
    slot = jnp.right_shift(iota((slots, n_lab), 0), 3)
    jj_of = jnp.where(slot < LIST + N_RELAY - 1, slot - (LIST - 1), slot - (LIST + N_RELAY - 2))
    far_a = lab_of(jnp.bitwise_and(jj_of, 1), -HOP - jnp.right_shift(jj_of, 1))
    far_b = lab_of(jnp.where(jj_of == N_RELAY - 1, 1, jnp.bitwise_and(jj_of, 1)), HOP + jnp.right_shift(jj_of, 1))
    source = jnp.where(slot < LIST + N_RELAY - 1, far_a, far_b)
    source = jnp.where(slot == N_NEAR, src_a, jnp.where(slot == N_NEAR + 1, src_b, source))
    source = jnp.where(slot < N_NEAR, lab_of(jnp.bitwise_and(slot, 1), jnp.right_shift(slot, 1) - (HOP - 1)), source)
    expand = (source == iota((slots, n_lab), 1)).astype(BF16)
    sel_lab = pick(jnp.where(blk_t > 0.5, 1.0, 0.0).astype(BF16), expand)
    blk_s = jnp.sum(jnp.where(sel_lab, mm(expand, blk_t.astype(BF16)), 0.0), axis=1, keepdims=True) - 1.0
    pc_s = jnp.sum(jnp.where(sel_lab, mm(expand, col_t.astype(BF16)), 0.0), axis=1, keepdims=True) - 1.0
    lane = iota((slots, BLOCK), 1)
    meta[...] = jnp.where(lane == 0, blk_s, pc_s)
    fwd_meta = remote(meta, meta_x, sx.at[0], rx.at[0], (partner, me))
    fwd_meta.start()
    for dz, dy in near:
        j = 2 * (dz + HOP - 1) + dy
        remote(sbuf.at[j], rbuf.at[2 * (HOP - 1 - dz) + dy], s1.at[0], rnear, (p, at(dy, dz))).start()
    rbuf[SELF_NEAR:SELF_NEAR + 1] = sbuf[SELF_NEAR:SELF_NEAR + 1]
    nbuf[N_NEAR:] = jnp.zeros((LIST - N_NEAR, cap, dim), BF16)
    rrbuf[0, N_RELAY:] = jnp.zeros((LIST - N_RELAY, cap, dim), BF16)
    rrbuf[1, N_RELAY:] = jnp.zeros((LIST - N_RELAY, cap, dim), BF16)

    def stop(s, jj):
        if jj == N_RELAY - 1:
            return (0, HOP) if s == 0 else (1, -HOP)
        m, dy = divmod(jj, 2)
        return dy, (m if s == 0 else -m)

    def far_slot(s, jj):
        return LIST + s * (N_RELAY - 1) + jj - 1

    srcs = (src_a, src_b)
    for s in range(2):
        chunk_out(s).wait_recv()
        out = mm(prel[s * width:(s + 1) * width], fbuf[s])
        relbuf[s] = out.reshape(LIST, cap, dim).astype(BF16)
        for jj in range(N_RELAY - 1, 0, -1):
            dy, dz = stop(s, jj)
            remote(relbuf.at[s, jj], rbuf.at[far_slot(s, jj)], sr.at[s], rfar, (p, at(dy, dz))).start()
        rbuf[N_NEAR + s:N_NEAR + s + 1] = relbuf[s, 0:1]

    def bulk(ref, sem):
        return remote(ref, ref, sem, sem, (partner, me))

    hrows = slots // 2
    hblk = nblk // 2
    first = core.astype(F32) * hblk
    lane_f = iota((hrows, BLOCK), 1).astype(F32)

    def slope128(x, w, b_of, pc, n):
        scores = mm(x, w, 1, 1)
        acc = jnp.zeros((hrows, BLOCK), F32)
        for b in range(n):
            acc = jnp.where(b_of == float(b), scores[:, b * BLOCK:(b + 1) * BLOCK], acc)
        return jax.nn.sigmoid(acc) - jnp.where(lane_f == pc, 1.0, 0.0)

    def spread(sl, b_of, n):
        return jnp.concatenate([jnp.where(b_of == float(b), sl, 0.0) for b in range(n)], axis=1).astype(BF16)

    def fwd_rows(hf):
        return remote(xall.at[pl.ds(hf * hrows, hrows)], xall.at[pl.ds(slots + hf * hrows, hrows)], sx.at[1 + hf], rx.at[1 + hf], (partner, me))

    def near_home():
        for dz, dy in near:
            remote(sbuf2.at[2 * (dz + HOP - 1) + dy], nbuf.at[2 * (HOP - 1 - dz) + dy], s2, rn, (p, at(dy, dz))).start()
        nbuf[SELF_NEAR:SELF_NEAR + 1] = sbuf2[SELF_NEAR:SELF_NEAR + 1]

    def own_rows(hf):
        x = rbuf[hf * LIST:(hf + 1) * LIST].astype(F32).reshape(hrows, dim).astype(BF16)
        xall[hf * hrows:(hf + 1) * hrows] = x
        fwd_rows(hf).start()
        if hf:
            near_home()
        b_of = meta[hf * hrows:(hf + 1) * hrows, 0:1]
        sl = slope128(x, w_ref[...], b_of, meta[hf * hrows:(hf + 1) * hrows, 1:2], nblk)
        slb[hf] = sl
        sall[hf * hrows:(hf + 1) * hrows] = spread(sl, b_of - first, hblk)

    def query_terms(hf):
        dq_part = mm(spread(slb[hf], meta[hf * hrows:(hf + 1) * hrows, 0:1], nblk), w_ref[...])
        sbuf2[hf * LIST:(hf + 1) * LIST] = dq_part.reshape(LIST, cap, dim).astype(BF16)

    def partner_rows(hf):
        at_row = slots + hf * hrows
        fwd_rows(hf).wait_recv()
        x = xall[at_row:at_row + hrows]
        b_of = meta_x[hf * hrows:(hf + 1) * hrows, 0:1] - first
        w_half = w_ref[pl.ds(pl.multiple_of(core * half, half), half), :]
        sl = slope128(x, w_half, b_of, meta_x[hf * hrows:(hf + 1) * hrows, 1:2], hblk)
        sall[at_row:at_row + hrows] = spread(sl, b_of, hblk)

    load_w.wait()
    bulk(rbuf.at[pl.ds(0, N_NEAR - 1)], rnear).wait_recv()
    own_rows(0)
    fwd_meta.wait_recv()
    partner_rows(0)
    query_terms(0)
    bulk(rbuf.at[pl.ds(LIST, LIST)], rfar).wait_recv()
    own_rows(1)
    query_terms(1)
    for s in range(2):
        for jj in range(N_RELAY - 1, 0, -1):
            dy, dz = stop(s, jj)
            remote(sbuf2.at[far_slot(s, jj)], rrbuf.at[s, jj], s2, rr.at[s], (p, at(dy, -dz))).start()
        rrbuf[s, 0:1] = sbuf2[N_NEAR + s:N_NEAR + s + 1]
    partner_rows(1)

    nx = chips // 2
    chip_h, chip_x = lax.div(chip, nx), lax.rem(chip, nx)

    def chip_at(dh, dx):
        return lax.rem(chip_h + dh, 2) * nx + lax.rem(chip_x + dx + nx, nx)

    ring = nx > 2
    others = [(1, 1), (1, -1), (0, 2), (0, 1), (0, -1)] if ring else [(1, dx) for dx in range(nx)] + [(0, dx) for dx in range(1, nx)]
    across = chip_at(1, 0)

    def to_across(g):
        return remote(dwbuf.at[g, across], dwrecv.at[g, chip], s3.at[g], r3.at[g], (2 * across + core, me))

    def corner(g):
        return remote(dwbuf.at[g, chip_at(1, 2)], comb.at[g], s3.at[g], r6.at[g], (2 * chip_at(0, 2) + core, me))

    for g in range(PARTS):
        dw = mm(sall[:, g * part:(g + 1) * part], xall[...], 0, 0)
        dwbuf[g] = dw.astype(BF16).reshape(chips, piece, dim)
        if ring:
            corner(g).start()
        for dh, dx in others:
            to = chip_at(dh, dx)
            remote(dwbuf.at[g, to], dwrecv.at[g, chip], s3.at[g], r3.at[g], (2 * to + core, me)).start()
        dwrecv[g, pl.ds(chip, 1)] = dwbuf[g, pl.ds(chip, 1)]

    if ring:
        for g in range(PARTS):
            corner(g).wait_recv()
            both = dwbuf[g, pl.ds(across, 1)].astype(F32) + comb[g:g + 1].astype(F32)
            dwbuf[g, pl.ds(across, 1)] = both.astype(BF16)
            to_across(g).start()

    def to_home(s):
        return remote(fsend.at[s], fback.at[s], sb.at[s], rb.at[s], (p, srcs[s]))

    def rows_of(c_, g, j):
        return pl.ds(pl.multiple_of(c_ * half + g * part + j * piece, piece), piece)

    def share(g, to, j):
        return remote(fin.at[g], wg_ref.at[rows_of(core, g, j)], s4.at[g], r4.at[g, j], (2 * to + core, me))

    direct = [(1, 0)] + ([(0, 2), (0, 1), (0, -1)] if ring else [(0, dx) for dx in range(1, nx)])
    passed = {(1, 0): [(0, 1), (0, -1)] if ring else [(0, dx) for dx in range(1, nx)], (0, 2): [(1, 0)]}
    second = [(1, 1), (1, -1), (1, 2)] if ring else [(1, dx) for dx in range(1, nx)]

    for g in range(PARTS):
        came = others + ([(1, 0)] if ring else [])
        bulk(dwrecv.at[g, pl.ds(0, len(came))], r3.at[g]).wait_recv()
        total = dwrecv[g, pl.ds(chip, 1)].astype(F32)
        for dh, dx in came:
            total = total + dwrecv[g, pl.ds(chip_at(dh, dx), 1)].astype(F32)
        done = (total[0] / n_pb).astype(BF16)
        fin[g] = done
        wg_ref[rows_of(core, g, chip), :] = done
        for dh, dx in direct:
            share(g, chip_at(dh, dx), chip).start()
        remote(fin.at[g], wg_ref.at[rows_of(core, g, chip)], s5, r5, (partner, me)).start()
        if g == 0:
            for s in range(2):
                bulk(rrbuf.at[s, pl.ds(0, N_RELAY - 1)], rr.at[s]).wait_recv()
                terms = rrbuf[s].astype(F32).reshape(width, dim).astype(BF16)
                fsend[s] = mm(prel[s * width:(s + 1) * width], terms, 0, 0).astype(BF16)
                to_home(s).start()

    def query_home():
        bulk(nbuf.at[pl.ds(0, N_NEAR - 1)], rn).wait_recv()
        terms = nbuf[...].astype(F32).reshape(width, dim).astype(BF16)
        home_sum = mm(pown[...], terms, 0, 0)
        for s in range(2):
            to_home(s).wait_recv()
            home_sum = home_sum + fback[s].astype(F32)
        dq_ref[...] = home_sum

    def arrived(g, dh, dx):
        owner = chip_at(dh, dx)
        share(g, owner, owner).wait_recv()
        there = wg_ref.at[rows_of(core, g, owner)]
        for fh, fx in passed.get((dh, dx), []):
            remote(there, there, s4.at[g], r4.at[g, owner], (2 * chip_at(fh, fx) + core, me)).start()
        remote(there, there, s5, r5, (partner, me)).start()

    for g in range(PARTS):
        for dh, dx in direct:
            arrived(g, dh, dx)
    for g in range(PARTS):
        for dh, dx in second:
            arrived(g, dh, dx)
    query_home()
    bulk(wg_ref.at[pl.ds(pl.multiple_of((1 - core) * half, half), half)], r5).wait_recv()

    bulk(sbuf.at[pl.ds(0, N_NEAR - 1)], s1.at[0]).wait_send()
    for s in range(2):
        chunk_out(s).wait_send()
        bulk(relbuf.at[s, pl.ds(0, N_RELAY - 1)], sr.at[s]).wait_send()
        to_home(s).wait_send()
        fwd_rows(s).wait_send()
    fwd_meta.wait_send()
    bulk(sbuf2.at[pl.ds(0, n_lab - 3)], s2).wait_send()
    for g in range(PARTS):
        bulk(dwbuf.at[g, pl.ds(0, chips - 1)], s3.at[g]).wait_send()
        bulk(dwbuf.at[g, pl.ds(0, chips - 1)], s4.at[g]).wait_send()
    bulk(wg_ref.at[pl.ds(pl.multiple_of(core * half, half), half)], s5).wait_send()


def write_out(a_ref, b_ref, oa_ref, ob_ref, sems):
    first = pltpu.make_async_copy(b_ref, ob_ref, sems.at[0])
    second = pltpu.make_async_copy(a_ref, oa_ref, sems.at[1])
    first.start()
    second.start()
    first.wait()
    second.wait()


def shards(n_pb, n_lab, queries, label_weights, sibling_blocks, positive_slot):
    rows, dim = queries.shape
    labels = label_weights.shape[0]
    kk = sibling_blocks.shape[1]
    cap = rows * kk // n_lab
    slots = n_lab * cap
    chips = n_pb // 2
    piece = labels // 2 // PARTS // chips
    width = LIST * cap
    sib = sibling_blocks.T
    pos = positive_slot.reshape(1, -1)
    vmem = pl.BlockSpec(memory_space=pltpu.VMEM)
    hbm = pl.BlockSpec(memory_space=pl.ANY)
    dma = pltpu.SemaphoreType.DMA

    def buf(*lead):
        return pltpu.VMEM((*lead, dim), BF16)

    dq, wg = pl.pallas_call(
        functools.partial(kernel, n_pb, n_lab),
        out_shape=(pltpu.VMEM((rows, dim), F32), pltpu.VMEM((labels, dim), BF16)),
        in_specs=[hbm] * 4,
        out_specs=(vmem, vmem),
        scratch_shapes=[
            buf(rows), pltpu.VMEM(sib.shape, jnp.int32), pltpu.VMEM(pos.shape, jnp.int32),
            buf(labels), buf(LIST, cap), buf(2, rows), buf(2, LIST, cap), buf(n_lab, cap), buf(2 * slots),
            pltpu.VMEM((2 * slots, labels // 2), BF16), pltpu.VMEM((2, slots // 2, BLOCK), F32),
            pltpu.VMEM((width, rows), BF16), pltpu.VMEM((2 * width, rows), BF16),
            pltpu.VMEM((slots, BLOCK), F32), pltpu.VMEM((slots, BLOCK), F32),
            buf(n_lab, cap), buf(LIST, cap), buf(2, LIST, cap), buf(2, rows), buf(2, rows),
            buf(PARTS, chips, piece), buf(PARTS, chips, piece), buf(PARTS, piece), buf(PARTS, piece),
            dma((3,)), dma, dma((1,)), dma, dma, dma((2,)), dma((2,)), dma((2,)), dma((3,)), dma((3,)), dma, dma, dma((2,)), dma((2,)), dma((2,)),
            dma((PARTS,)), dma((PARTS,)), dma((PARTS,)), dma((PARTS, chips)), dma, dma, dma((PARTS,)),
        ],
        compiler_params=pltpu.CompilerParams(collective_id=0, has_side_effects=True),
    )(queries, label_weights, sib, pos)
    near = functools.partial(pltpu.with_memory_space_constraint, memory_space=pltpu.VMEM)
    return pl.pallas_call(
        write_out,
        out_shape=(jax.ShapeDtypeStruct((rows, dim), F32), jax.ShapeDtypeStruct((labels, dim), BF16)),
        in_specs=[vmem, vmem],
        out_specs=(hbm, hbm),
        scratch_shapes=[dma((2,))],
    )(near(dq), near(wg))


def solution(mesh):
    in_specs = (P(("pb", "lab"), None), P("lab", None), P("pb", None), P("pb"))
    out_specs = (P(("pb", "lab"), None), P("lab", None))
    body = functools.partial(shards, mesh.shape["pb"], mesh.shape["lab"])
    return jax.shard_map(body, mesh=mesh, in_specs=in_specs, out_specs=out_specs, check_vma=False)
```

```python
import functools

import jax
import jax.numpy as jnp
from jax import lax
from jax.experimental import pallas as pl
from jax.experimental.pallas import tpu as pltpu
from jax.sharding import PartitionSpec as P

MESH = pl.DeviceIdType.MESH
BLOCK = 128
HOP = 4
LIST = 16
PARTS = 2
F32 = jnp.float32
BF16 = jnp.bfloat16
SELF_NEAR = 2 * (HOP - 1)
N_NEAR = 2 * (2 * HOP - 1)
N_RELAY = 2 * HOP + 1


def mm(a, b, ca=1, cb=0):
    return lax.dot_general(a, b, (((ca,), (cb,)), ((), ())), preferred_element_type=F32)


def iota(shape, ax):
    return lax.broadcasted_iota(jnp.int32, shape, ax)


def kernel(n_pb, n_lab, q_hbm, w_hbm, sib_hbm, pos_hbm, dq_ref, wg_ref, q_ref, sib_ref, pos_ref, w_ref, sbuf, fbuf, relbuf, rbuf, xall, sall, slb, pown, prel, meta, meta_x,
           sbuf2, nbuf, rrbuf, fsend, fback, dwbuf, dwrecv, comb, fin, dwacc,
           sq, sw, s1, rnear, rfar, sf, rf, sr, sx, rx, s2, rn, rr, sb, rb, s3, r3, s4, r4, s5, r5, r6):
    kk, total_rows = sib_hbm.shape
    rows, dim = q_hbm.shape
    cap = rows * kk // n_lab
    slots = n_lab * cap
    labels = w_hbm.shape[0]
    nblk = labels // BLOCK
    half = labels // 2
    chips = n_pb // 2
    part = half // PARTS
    piece = part // chips
    nz = n_lab // 2
    p = lax.axis_index("pb")
    me = lax.axis_index("lab")
    core = lax.rem(p, 2)
    chip = lax.div(p, 2)
    partner = p + 1 - 2 * core
    my_y = lax.div(me, nz)
    my_z = lax.rem(me, nz)

    def at(dy, dz):
        return lax.rem(my_y + dy, 2) * nz + lax.rem(my_z + dz + nz, nz)

    loads = [
        pltpu.make_async_copy(src, dst, sq.at[n])
        for n, (src, dst) in enumerate(((sib_hbm, sib_ref), (q_hbm, q_ref), (pos_hbm, pos_ref)))
    ]
    for load in loads:
        load.start()
    load_w = pltpu.make_async_copy(w_hbm, w_ref, sw)
    load_w.start()

    barrier = pltpu.get_barrier_semaphore()
    for dz in sorted(range(-HOP, HOP + 1), key=abs, reverse=True):
        for dy in (1, 0):
            if dz or dy:
                pl.semaphore_signal(barrier, inc=1, device_id=(p, at(dy, dz)), device_id_type=MESH)
    pl.semaphore_signal(barrier, inc=1, device_id=(partner, me), device_id_type=MESH)
    for t in range(1, chips):
        pl.semaphore_signal(barrier, inc=1, device_id=(2 * lax.rem(chip + t, chips) + core, me), device_id_type=MESH)

    src_a, src_b = at(0, -HOP), at(0, HOP)
    upper = (iota((rows, rows), 0) <= iota((rows, rows), 1)).astype(BF16)

    def pick(hit_b, expand):
        want = (lax.rem(iota((expand.shape[0], rows), 0), cap) + 1).astype(F32)
        rank = mm(hit_b, upper)
        on = mm(expand, hit_b)
        return jnp.logical_and(on > 0.5, mm(expand, rank.astype(BF16)) == want)

    for load in loads:
        load.wait()
    sib = sib_ref[...]
    col = iota((total_rows, 3 * rows), 1)
    run_of = jnp.where(col < rows, me, jnp.where(col < 2 * rows, src_a, src_b))
    take = (iota((total_rows, 3 * rows), 0) == run_of * rows + lax.rem(col, rows)).astype(BF16)
    mine3 = mm(sib.astype(BF16), take)

    jrow = iota((LIST, rows), 0)
    jy = lax.rem(jrow, 2)
    jm = lax.div(jrow, 2)

    def lab_of(dy, dz):
        return lax.rem(my_y + dy, 2) * nz + lax.rem(my_z + dz + nz, nz)

    near_ids = jnp.where(jrow < N_NEAR, lab_of(jy, jm - (HOP - 1)), -1)
    ids_a = jnp.where(jrow < N_RELAY, lab_of(jy, jm), -1)
    ids_b = jnp.where(jrow < N_RELAY, lab_of(jnp.where(jrow == N_RELAY - 1, 1, jy), -jm), -1)
    hits = []
    for n, ids in enumerate((near_ids, ids_a, ids_b)):
        hit = jnp.zeros((LIST, rows), F32)
        for k in range(kk):
            blocks = mine3[k:k + 1, n * rows:(n + 1) * rows].astype(jnp.int32)
            hit = jnp.where(jnp.right_shift(blocks, 3) == ids, 1.0, hit)
        hits.append(hit)
    lists = 3 * LIST
    sel3 = pick(jnp.concatenate(hits, axis=0).astype(BF16), (iota((lists * cap, lists), 0) // cap == iota((lists * cap, lists), 1)).astype(BF16))
    sel3 = jnp.where(sel3, 1.0, 0.0).astype(BF16)
    width = LIST * cap
    pown[...] = sel3[:width]
    prel[...] = sel3[width:]
    sbuf[...] = mm(sel3[:width], q_ref[...]).reshape(LIST, cap, dim).astype(BF16)

    pl.semaphore_wait(barrier, 2 * (2 * HOP + 1) - 1 + chips)

    def remote(src, dst, send, recv, dev):
        return pltpu.make_async_remote_copy(
            src_ref=src, dst_ref=dst, send_sem=send, recv_sem=recv, device_id=dev, device_id_type=MESH)

    def chunk_out(s):
        return remote(q_ref, fbuf.at[s], sf.at[s], rf.at[s], (p, at(0, HOP if s == 0 else -HOP)))

    chunk_out(0).start()
    chunk_out(1).start()
    near = [(dz * sg, dy) for dz in range(HOP - 1, -1, -1) for sg in ((1, -1) if dz else (1,)) for dy in (0, 1) if dz or dy]

    qrow = iota((n_lab, total_rows), 1)
    in_run = jnp.right_shift(qrow, 5) == iota((n_lab, total_rows), 0)
    fold = (jnp.bitwise_and(iota((total_rows, rows), 0), rows - 1) == iota((total_rows, rows), 1)).astype(BF16)
    here = jnp.right_shift(sib, 3) == me
    pos = pos_ref[...]
    blk1 = jnp.sum(jnp.where(here, jnp.bitwise_and(sib, 7) + 1, 0), axis=0, keepdims=True)
    is_pos = jnp.logical_and(here, iota((kk, total_rows), 0) == jnp.right_shift(pos, 7))
    col1 = jnp.sum(jnp.where(is_pos, jnp.bitwise_and(pos, BLOCK - 1) + 1, 0), axis=0, keepdims=True)
    packed = jnp.concatenate([jnp.where(in_run, blk1, 0), jnp.where(in_run, col1, 0)], axis=0)
    table = mm(packed.astype(F32).astype(BF16), fold)
    blk_t, col_t = table[:n_lab], table[n_lab:]
    slot = jnp.right_shift(iota((slots, n_lab), 0), 3)
    jj_of = jnp.where(slot < LIST + N_RELAY - 1, slot - (LIST - 1), slot - (LIST + N_RELAY - 2))
    far_a = lab_of(jnp.bitwise_and(jj_of, 1), -HOP - jnp.right_shift(jj_of, 1))
    far_b = lab_of(jnp.where(jj_of == N_RELAY - 1, 1, jnp.bitwise_and(jj_of, 1)), HOP + jnp.right_shift(jj_of, 1))
    source = jnp.where(slot < LIST + N_RELAY - 1, far_a, far_b)
    source = jnp.where(slot == N_NEAR, src_a, jnp.where(slot == N_NEAR + 1, src_b, source))
    source = jnp.where(slot < N_NEAR, lab_of(jnp.bitwise_and(slot, 1), jnp.right_shift(slot, 1) - (HOP - 1)), source)
    expand = (source == iota((slots, n_lab), 1)).astype(BF16)
    sel_lab = pick(jnp.where(blk_t > 0.5, 1.0, 0.0).astype(BF16), expand)
    blk_s = jnp.sum(jnp.where(sel_lab, mm(expand, blk_t.astype(BF16)), 0.0), axis=1, keepdims=True) - 1.0
    pc_s = jnp.sum(jnp.where(sel_lab, mm(expand, col_t.astype(BF16)), 0.0), axis=1, keepdims=True) - 1.0
    lane = iota((slots, BLOCK), 1)
    meta[...] = jnp.where(lane == 0, blk_s, pc_s)
    fwd_meta = remote(meta, meta_x, sx.at[0], rx.at[0], (partner, me))
    fwd_meta.start()
    for dz, dy in near:
        j = 2 * (dz + HOP - 1) + dy
        remote(sbuf.at[j], rbuf.at[2 * (HOP - 1 - dz) + dy], s1.at[0], rnear, (p, at(dy, dz))).start()
    rbuf[SELF_NEAR:SELF_NEAR + 1] = sbuf[SELF_NEAR:SELF_NEAR + 1]
    nbuf[N_NEAR:] = jnp.zeros((LIST - N_NEAR, cap, dim), BF16)
    rrbuf[0, N_RELAY:] = jnp.zeros((LIST - N_RELAY, cap, dim), BF16)
    rrbuf[1, N_RELAY:] = jnp.zeros((LIST - N_RELAY, cap, dim), BF16)

    def stop(s, jj):
        if jj == N_RELAY - 1:
            return (0, HOP) if s == 0 else (1, -HOP)
        m, dy = divmod(jj, 2)
        return dy, (m if s == 0 else -m)

    def far_slot(s, jj):
        return LIST + s * (N_RELAY - 1) + jj - 1

    srcs = (src_a, src_b)
    for s in range(2):
        chunk_out(s).wait_recv()
        out = mm(prel[s * width:(s + 1) * width], fbuf[s])
        relbuf[s] = out.reshape(LIST, cap, dim).astype(BF16)
        for jj in range(N_RELAY - 1, 0, -1):
            dy, dz = stop(s, jj)
            remote(relbuf.at[s, jj], rbuf.at[far_slot(s, jj)], sr.at[s], rfar, (p, at(dy, dz))).start()
        rbuf[N_NEAR + s:N_NEAR + s + 1] = relbuf[s, 0:1]

    def bulk(ref, sem):
        return remote(ref, ref, sem, sem, (partner, me))

    hrows = slots // 2
    hblk = nblk // 2
    first = core.astype(F32) * hblk
    lane_f = iota((hrows, BLOCK), 1).astype(F32)

    def slope128(x, w, b_of, pc, n):
        scores = mm(x, w, 1, 1)
        acc = jnp.zeros((hrows, BLOCK), F32)
        for b in range(n):
            acc = jnp.where(b_of == float(b), scores[:, b * BLOCK:(b + 1) * BLOCK], acc)
        return jax.nn.sigmoid(acc) - jnp.where(lane_f == pc, 1.0, 0.0)

    def spread(sl, b_of, n):
        return jnp.concatenate([jnp.where(b_of == float(b), sl, 0.0) for b in range(n)], axis=1).astype(BF16)

    def fwd_rows(hf):
        return remote(xall.at[pl.ds(2 * hf * hrows, hrows)], xall.at[pl.ds((2 * hf + 1) * hrows, hrows)], sx.at[1 + hf], rx.at[1 + hf], (partner, me))

    def near_home():
        for dz, dy in near:
            remote(sbuf2.at[2 * (dz + HOP - 1) + dy], nbuf.at[2 * (HOP - 1 - dz) + dy], s2, rn, (p, at(dy, dz))).start()
        nbuf[SELF_NEAR:SELF_NEAR + 1] = sbuf2[SELF_NEAR:SELF_NEAR + 1]

    def own_rows(hf):
        x = rbuf[hf * LIST:(hf + 1) * LIST].astype(F32).reshape(hrows, dim).astype(BF16)
        xall[2 * hf * hrows:(2 * hf + 1) * hrows] = x
        fwd_rows(hf).start()
        if hf:
            near_home()
        b_of = meta[hf * hrows:(hf + 1) * hrows, 0:1]
        sl = slope128(x, w_ref[...], b_of, meta[hf * hrows:(hf + 1) * hrows, 1:2], nblk)
        slb[hf] = sl
        sall[2 * hf * hrows:(2 * hf + 1) * hrows] = spread(sl, b_of - first, hblk)

    def query_terms(hf):
        dq_part = mm(spread(slb[hf], meta[hf * hrows:(hf + 1) * hrows, 0:1], nblk), w_ref[...])
        sbuf2[hf * LIST:(hf + 1) * LIST] = dq_part.reshape(LIST, cap, dim).astype(BF16)

    def partner_rows(hf):
        at_row = (2 * hf + 1) * hrows
        fwd_rows(hf).wait_recv()
        x = xall[at_row:at_row + hrows]
        b_of = meta_x[hf * hrows:(hf + 1) * hrows, 0:1] - first
        w_half = w_ref[pl.ds(pl.multiple_of(core * half, half), half), :]
        sl = slope128(x, w_half, b_of, meta_x[hf * hrows:(hf + 1) * hrows, 1:2], hblk)
        sall[at_row:at_row + hrows] = spread(sl, b_of, hblk)

    load_w.wait()
    bulk(rbuf.at[pl.ds(0, N_NEAR - 1)], rnear).wait_recv()
    own_rows(0)
    fwd_meta.wait_recv()
    partner_rows(0)
    query_terms(0)
    for g in range(PARTS):
        dwacc[g] = mm(sall[:slots, g * part:(g + 1) * part], xall[:slots], 0, 0)
    bulk(rbuf.at[pl.ds(LIST, LIST)], rfar).wait_recv()
    own_rows(1)
    query_terms(1)
    for s in range(2):
        for jj in range(N_RELAY - 1, 0, -1):
            dy, dz = stop(s, jj)
            remote(sbuf2.at[far_slot(s, jj)], rrbuf.at[s, jj], s2, rr.at[s], (p, at(dy, -dz))).start()
        rrbuf[s, 0:1] = sbuf2[N_NEAR + s:N_NEAR + s + 1]
    partner_rows(1)

    nx = chips // 2
    chip_h, chip_x = lax.div(chip, nx), lax.rem(chip, nx)

    def chip_at(dh, dx):
        return lax.rem(chip_h + dh, 2) * nx + lax.rem(chip_x + dx + nx, nx)

    ring = nx > 2
    others = [(1, 1), (1, -1), (0, 2), (0, 1), (0, -1)] if ring else [(1, dx) for dx in range(nx)] + [(0, dx) for dx in range(1, nx)]
    across = chip_at(1, 0)

    def to_across(g):
        return remote(dwbuf.at[g, across], dwrecv.at[g, chip], s3.at[g], r3.at[g], (2 * across + core, me))

    def corner(g):
        return remote(dwbuf.at[g, chip_at(1, 2)], comb.at[g], s3.at[g], r6.at[g], (2 * chip_at(0, 2) + core, me))

    for g in range(PARTS):
        dw = dwacc[g] + mm(sall[slots:, g * part:(g + 1) * part], xall[slots:], 0, 0)
        dwbuf[g] = dw.astype(BF16).reshape(chips, piece, dim)
        if ring:
            corner(g).start()
        for dh, dx in others:
            to = chip_at(dh, dx)
            remote(dwbuf.at[g, to], dwrecv.at[g, chip], s3.at[g], r3.at[g], (2 * to + core, me)).start()
        dwrecv[g, pl.ds(chip, 1)] = dwbuf[g, pl.ds(chip, 1)]

    if ring:
        for g in range(PARTS):
            corner(g).wait_recv()
            both = dwbuf[g, pl.ds(across, 1)].astype(F32) + comb[g:g + 1].astype(F32)
            dwbuf[g, pl.ds(across, 1)] = both.astype(BF16)
            to_across(g).start()

    def to_home(s):
        return remote(fsend.at[s], fback.at[s], sb.at[s], rb.at[s], (p, srcs[s]))

    def rows_of(c_, g, j):
        return pl.ds(pl.multiple_of(c_ * half + g * part + j * piece, piece), piece)

    def share(g, to, j):
        return remote(fin.at[g], wg_ref.at[rows_of(core, g, j)], s4.at[g], r4.at[g, j], (2 * to + core, me))

    direct = [(1, 0)] + ([(0, 2), (0, 1), (0, -1)] if ring else [(0, dx) for dx in range(1, nx)])
    passed = {(1, 0): [(0, 1), (0, -1)] if ring else [(0, dx) for dx in range(1, nx)], (0, 2): [(1, 0)]}
    second = [(1, 1), (1, -1), (1, 2)] if ring else [(1, dx) for dx in range(1, nx)]

    for g in range(PARTS):
        came = others + ([(1, 0)] if ring else [])
        bulk(dwrecv.at[g, pl.ds(0, len(came))], r3.at[g]).wait_recv()
        total = dwrecv[g, pl.ds(chip, 1)].astype(F32)
        for dh, dx in came:
            total = total + dwrecv[g, pl.ds(chip_at(dh, dx), 1)].astype(F32)
        done = (total[0] / n_pb).astype(BF16)
        fin[g] = done
        wg_ref[rows_of(core, g, chip), :] = done
        for dh, dx in direct:
            share(g, chip_at(dh, dx), chip).start()
        remote(fin.at[g], wg_ref.at[rows_of(core, g, chip)], s5, r5, (partner, me)).start()
        if g == PARTS - 1:
            for s in range(2):
                bulk(rrbuf.at[s, pl.ds(0, N_RELAY - 1)], rr.at[s]).wait_recv()
                terms = rrbuf[s].astype(F32).reshape(width, dim).astype(BF16)
                fsend[s] = mm(prel[s * width:(s + 1) * width], terms, 0, 0).astype(BF16)
                to_home(s).start()

    def query_home():
        bulk(nbuf.at[pl.ds(0, N_NEAR - 1)], rn).wait_recv()
        terms = nbuf[...].astype(F32).reshape(width, dim).astype(BF16)
        home_sum = mm(pown[...], terms, 0, 0)
        for s in range(2):
            to_home(s).wait_recv()
            home_sum = home_sum + fback[s].astype(F32)
        dq_ref[...] = home_sum

    def arrived(g, dh, dx):
        owner = chip_at(dh, dx)
        share(g, owner, owner).wait_recv()
        there = wg_ref.at[rows_of(core, g, owner)]
        for fh, fx in passed.get((dh, dx), []):
            remote(there, there, s4.at[g], r4.at[g, owner], (2 * chip_at(fh, fx) + core, me)).start()
        remote(there, there, s5, r5, (partner, me)).start()

    for g in range(PARTS):
        for dh, dx in direct:
            arrived(g, dh, dx)
    for g in range(PARTS):
        for dh, dx in second:
            arrived(g, dh, dx)
    query_home()
    bulk(wg_ref.at[pl.ds(pl.multiple_of((1 - core) * half, half), half)], r5).wait_recv()

    bulk(sbuf.at[pl.ds(0, N_NEAR - 1)], s1.at[0]).wait_send()
    for s in range(2):
        chunk_out(s).wait_send()
        bulk(relbuf.at[s, pl.ds(0, N_RELAY - 1)], sr.at[s]).wait_send()
        to_home(s).wait_send()
        fwd_rows(s).wait_send()
    fwd_meta.wait_send()
    bulk(sbuf2.at[pl.ds(0, n_lab - 3)], s2).wait_send()
    for g in range(PARTS):
        bulk(dwbuf.at[g, pl.ds(0, chips - 1)], s3.at[g]).wait_send()
        bulk(dwbuf.at[g, pl.ds(0, chips - 1)], s4.at[g]).wait_send()
    bulk(wg_ref.at[pl.ds(pl.multiple_of(core * half, half), half)], s5).wait_send()


def write_out(a_ref, b_ref, oa_ref, ob_ref, sems):
    first = pltpu.make_async_copy(b_ref, ob_ref, sems.at[0])
    second = pltpu.make_async_copy(a_ref, oa_ref, sems.at[1])
    first.start()
    second.start()
    first.wait()
    second.wait()


def shards(n_pb, n_lab, queries, label_weights, sibling_blocks, positive_slot):
    rows, dim = queries.shape
    labels = label_weights.shape[0]
    kk = sibling_blocks.shape[1]
    cap = rows * kk // n_lab
    slots = n_lab * cap
    chips = n_pb // 2
    piece = labels // 2 // PARTS // chips
    width = LIST * cap
    sib = sibling_blocks.T
    pos = positive_slot.reshape(1, -1)
    vmem = pl.BlockSpec(memory_space=pltpu.VMEM)
    hbm = pl.BlockSpec(memory_space=pl.ANY)
    dma = pltpu.SemaphoreType.DMA

    def buf(*lead):
        return pltpu.VMEM((*lead, dim), BF16)

    dq, wg = pl.pallas_call(
        functools.partial(kernel, n_pb, n_lab),
        out_shape=(pltpu.VMEM((rows, dim), F32), pltpu.VMEM((labels, dim), BF16)),
        in_specs=[hbm] * 4,
        out_specs=(vmem, vmem),
        scratch_shapes=[
            buf(rows), pltpu.VMEM(sib.shape, jnp.int32), pltpu.VMEM(pos.shape, jnp.int32),
            buf(labels), buf(LIST, cap), buf(2, rows), buf(2, LIST, cap), buf(n_lab, cap), buf(2 * slots),
            pltpu.VMEM((2 * slots, labels // 2), BF16), pltpu.VMEM((2, slots // 2, BLOCK), F32),
            pltpu.VMEM((width, rows), BF16), pltpu.VMEM((2 * width, rows), BF16),
            pltpu.VMEM((slots, BLOCK), F32), pltpu.VMEM((slots, BLOCK), F32),
            buf(n_lab, cap), buf(LIST, cap), buf(2, LIST, cap), buf(2, rows), buf(2, rows),
            buf(PARTS, chips, piece), buf(PARTS, chips, piece), buf(PARTS, piece), buf(PARTS, piece),
            pltpu.VMEM((PARTS, labels // 2 // PARTS, dim), F32),
            dma((3,)), dma, dma((1,)), dma, dma, dma((2,)), dma((2,)), dma((2,)), dma((3,)), dma((3,)), dma, dma, dma((2,)), dma((2,)), dma((2,)),
            dma((PARTS,)), dma((PARTS,)), dma((PARTS,)), dma((PARTS, chips)), dma, dma, dma((PARTS,)),
        ],
        compiler_params=pltpu.CompilerParams(collective_id=0, has_side_effects=True),
    )(queries, label_weights, sib, pos)
    near = functools.partial(pltpu.with_memory_space_constraint, memory_space=pltpu.VMEM)
    return pl.pallas_call(
        write_out,
        out_shape=(jax.ShapeDtypeStruct((rows, dim), F32), jax.ShapeDtypeStruct((labels, dim), BF16)),
        in_specs=[vmem, vmem],
        out_specs=(hbm, hbm),
        scratch_shapes=[dma((2,))],
    )(near(dq), near(wg))


def solution(mesh):
    in_specs = (P(("pb", "lab"), None), P("lab", None), P("pb", None), P("pb"))
    out_specs = (P(("pb", "lab"), None), P("lab", None))
    body = functools.partial(shards, mesh.shape["pb"], mesh.shape["lab"])
    return jax.shard_map(body, mesh=mesh, in_specs=in_specs, out_specs=out_specs, check_vma=False)
```
